128 devices in a mesh: ty: 4 (over x_hi, core), tx: 8 (over y, x_lo), ta: 4 (over z).
Axes of the slice: x: 4 (x_hi: 2, x_lo: 2; x = x_hi * 2 + x_lo), y: 4, z: 4, core: 2. Of those that a mesh axis runs over, the one named last changes fastest.
Arguments:
- movie: bfloat16 [16, 4, 1024, 1024], P('ta', None, 'ty', 'tx'), may hold values from 0 to 2
- footprints: float32 [2048, 4096], P(('ty', 'tx')), may hold values from 0 to 1
- traces: float32 [16, 2048], P('ta', ('ty', 'tx')), may hold values from 0 to 1
- anchor_row: int32 [2048], P(('ty', 'tx')), may hold values from -1 to 15
- anchor_col: int32 [2048], P(('ty', 'tx')), may hold values from -1 to 7
Outputs:
- footprints_out: float32 [2048, 4096], P(('ty', 'tx'))
- traces_out: float32 [16, 2048], P('ta', ('ty', 'tx'))
The draws below stay inside these ranges and needn't reach their ends.
Inputs may be any that keep to these rules, and one draw needn't show every extreme that they name: `anchor_row`: cell row within the owner tile at which a neuron's patch block starts; -1 puts its upper half into the tile above. `anchor_col`: cell column within the owner tile at which a neuron's patch block starts; -1 puts its left half into the tile beside it.
All inputs are finite; a program needn't handle non-finite values.
Results may differ from the reference program's by a relative error of at most 0.0003.
Values may be sent and summed in bfloat16 or wider, within the bound.
No kernel may reach another device: no remote copies, remote signals or barrier semaphores. Data moves between devices by JAX's collectives and lax.ppermute only.
A program may use at most 128 MiB of HBM per device.

```python
import jax
import jax.numpy as jnp
from jax import lax

CELL = 16
PZ = 4
CY = 16
CX = 8
K_DEV = 64
ITERS = 2
PATCH = 4096
NEURONS = 2048
FRAMES = 16
NY = 1024
NX = 1024
N_TX = 8


def set_ends(entries, rng, least, high):
    index_at = [jax.random.randint(jax.random.fold_in(rng, axis), (), 0, length) for axis, length in enumerate(entries.shape)]
    main_axis = entries.shape.index(max(entries.shape))
    beside = index_at[:main_axis] + [(index_at[main_axis] + 1) % entries.shape[main_axis]] + index_at[main_axis + 1:]
    return entries.at[tuple(index_at)].set(least).at[tuple(beside)].set(high)


def shard_levels(own_key, shape, split, smallest, largest):
    loudness = 1.0
    for axis_at, shards_of in split:
        steps = jax.random.uniform(jax.random.fold_in(jax.random.fold_in(own_key, 6), axis_at), (shards_of,), jnp.float32, smallest / len(split), largest / len(split))
        loudness = loudness * jnp.repeat(jnp.exp(steps), shape[axis_at] // shards_of).reshape((-1,) + (1,) * (len(shape) - 1 - axis_at))
    return loudness


def setup_inputs(seed: int = 0) -> dict:
    streams_of = jax.random.split(jax.random.key(seed), 6)
    return {
        "movie": jnp.clip(2.0 * jax.random.uniform(streams_of[0], (FRAMES, PZ, NY, NX), jnp.float32) ** shard_levels(streams_of[0], (FRAMES, PZ, NY, NX), ((0, 4), (2, 4), (3, 8)), -0.2, 0.2), 0.0, 2.0).astype(jnp.bfloat16),
        "footprints": jnp.clip(1.0 * jax.random.uniform(streams_of[1], (NEURONS, PATCH), jnp.float32) ** shard_levels(streams_of[1], (NEURONS, PATCH), ((0, 32),), -0.2, 0.2), 0.0, 1.0),
        "traces": jnp.clip(1.0 * jax.random.uniform(streams_of[2], (FRAMES, NEURONS), jnp.float32) ** shard_levels(streams_of[2], (FRAMES, NEURONS), ((0, 4), (1, 32)), -0.2, 0.2), 0.0, 1.0),
        "anchor_row": set_ends(jax.random.randint(streams_of[3], (NEURONS,), -1, CY), jax.random.fold_in(streams_of[3], 1), -1, CY - 1).astype(jnp.int32),
        "anchor_col": set_ends(jax.random.randint(streams_of[4], (NEURONS,), -1, CX), jax.random.fold_in(streams_of[4], 1), -1, CX - 1).astype(jnp.int32),
    }


RIDGE = 1.0


def cell_lists(anchor_row, anchor_col):
    neuron_ids = jnp.arange(NEURONS, dtype=jnp.int32)
    tile_row = neuron_ids // (K_DEV * N_TX)
    tile_col = (neuron_ids // K_DEV) % N_TX
    grid_cols = CX * N_TX + 2
    top_cell = tile_row * CY + anchor_row.astype(jnp.int32) + 1
    left_cell = tile_col * CX + anchor_col.astype(jnp.int32) + 1
    corner = top_cell * grid_cols + left_cell
    offsets = jnp.array([0, 1, grid_cols, grid_cols + 1], dtype=jnp.int32)
    return (corner[:, None] + offsets[None, :]).reshape(-1)


def frame_cells(movie_frame):
    padded = jnp.pad(movie_frame.astype(jnp.float32), ((0, 0), (CELL, CELL), (CELL, CELL)))
    grid_rows = NY // CELL + 2
    grid_cols = NX // CELL + 2
    blocks = padded.reshape(PZ, grid_rows, CELL, grid_cols, CELL).transpose(1, 3, 0, 2, 4)
    return blocks.reshape(grid_rows * grid_cols, PZ * CELL * CELL)


def frame_residue(movie_frame, trace_row, footprints, cell_ids, cell_total):
    products = footprints.reshape(NEURONS, 4, PZ * CELL * CELL) * trace_row[:, None, None]
    estimate = jax.ops.segment_sum(products.reshape(NEURONS * 4, -1), cell_ids, num_segments=cell_total)
    residue = frame_cells(movie_frame) - estimate
    return jnp.take(residue, cell_ids, axis=0).reshape(NEURONS, PATCH)


def reference(movie, footprints, traces, anchor_row, anchor_col):
    cell_ids = cell_lists(anchor_row, anchor_col)
    cell_total = (NY // CELL + 2) * (NX // CELL + 2)
    for sweep in range(ITERS):
        energy = jnp.sum(footprints * footprints, axis=1)

        def trace_frame(inputs):
            movie_frame, trace_row = inputs
            gathered = frame_residue(movie_frame, trace_row, footprints, cell_ids, cell_total)
            update = jnp.sum(footprints * gathered, axis=1)
            return jnp.maximum(trace_row + update / (energy + RIDGE), 0.0)

        traces = lax.map(trace_frame, (movie, traces))

        def foot_frame(running, inputs):
            movie_frame, trace_row = inputs
            gathered = frame_residue(movie_frame, trace_row, footprints, cell_ids, cell_total)
            return running + trace_row[:, None] * gathered, None

        numerator, _ = lax.scan(foot_frame, jnp.zeros((NEURONS, PATCH), jnp.float32), (movie, traces))
        strength = jnp.sum(traces * traces, axis=0)
        footprints = jnp.maximum(footprints + numerator / (strength + RIDGE)[:, None], 0.0)
    return footprints, traces
```

```python
import functools

import jax
import jax.numpy as jnp
from jax import lax
from jax.experimental import pallas as pl
from jax.experimental.pallas import tpu as pltpu
from jax.sharding import PartitionSpec as P

ITERS = 2
RIDGE = 1.0
TX = 8
TA = 4
GROUP = TX * TA
OWNED = 64
COUNT = TX * OWNED
ROW = (TX * 8 + 2) * TA
CELL_ROWS = 16
FIELD = (CELL_ROWS + 2) * ROW
INNER = CELL_ROWS * ROW
VMEM = pl.BlockSpec(memory_space=pltpu.VMEM)
SMEM = pl.BlockSpec(memory_space=pltpu.SMEM)
F32 = jnp.float32


def iotas():
    return (
        lax.broadcasted_iota(jnp.int32, (8, 128), 0),
        lax.broadcasted_iota(jnp.int32, (8, 128), 1),
    )


def pick_lanes(value, index):
    return jnp.take_along_axis(value, index, axis=1, mode="promise_in_bounds")


def pick_rows(value, index):
    return jnp.take_along_axis(value, index, axis=0, mode="promise_in_bounds")


def merge_lanes(first, second, shift, lane):
    return jnp.where(
        (lane & shift) != 0,
        second + pltpu.roll(second, shift, 1),
        first + pltpu.roll(first, 128 - shift, 1),
    )


def merge_rows(first, second, shift, sub):
    return jnp.where(
        (sub & shift) != 0,
        second + pltpu.roll(second, shift, 0),
        first + pltpu.roll(first, 8 - shift, 0),
    )


def spread(value, m, sub, lane):
    wide = pick_lanes(value, (lane & 96) + m)
    turned = pltpu.roll(wide, 4, 0)
    low = sub < 4
    return jnp.where(low, wide, turned), jnp.where(low, turned, wide)


def print_pair(prints_ref, neuron, sub, lane):
    row = jnp.broadcast_to(prints_ref[pl.ds(neuron, 1), :], (8, 128))
    index = (lane & 31) + jnp.where(sub < 4, 0, 32)
    return pick_lanes(row, index), pick_lanes(row, index + 64)


def patch(neuron, places_ref):
    start = pl.multiple_of(places_ref[neuron], 4)
    return pl.ds(start, 8), pl.ds(start + ROW, 8)


def subtract_all(activity_ref, prints_ref, places_ref, field_ref):
    sub, lane = iotas()

    def tile(v, _):
        value = activity_ref[v]

        def some(mh, _):
            for ml in range(4):
                pair = spread(value, mh * 4 + ml, sub, lane)
                for half in range(2):
                    neuron = v * OWNED + mh * 8 + half * 4 + ml
                    upper, lower = print_pair(prints_ref, neuron, sub, lane)
                    top, bottom = patch(neuron, places_ref)
                    field_ref[top, :] -= pair[half] * upper
                    field_ref[bottom, :] -= pair[half] * lower
            return 0

        return lax.fori_loop(0, 8, some, 0)

    lax.fori_loop(0, TX, tile, 0)


def start_field(movie_ref, field_ref):
    field_ref[0:ROW, :] = jnp.zeros((ROW, 128), F32)
    field_ref[ROW + INNER :, :] = jnp.zeros((ROW, 128), F32)

    def one(r, _):
        field_ref[pl.ds((r + 1) * ROW, ROW), :] = movie_ref[pl.ds(r * ROW, ROW), :]
        return 0

    lax.fori_loop(0, CELL_ROWS, one, 0)


def add_halo(field_ref, above_ref, below_ref, whole_ref):
    whole_ref[0 : 2 * ROW, :] = field_ref[0 : 2 * ROW, :] + above_ref[...]

    def one(r, _):
        whole_ref[pl.ds(r * ROW, ROW), :] = field_ref[pl.ds(r * ROW, ROW), :]
        return 0

    lax.fori_loop(2, CELL_ROWS, one, 0)
    whole_ref[INNER:, :] = field_ref[INNER:, :] + below_ref[...]


def pack_kernel(rows_ref, tail_ref, out_ref):
    lane = lax.broadcasted_iota(jnp.int32, (16, 128), 1)
    for a in range(8):
        parts = [rows_ref[:, d * 1024 + a * 128 : d * 1024 + a * 128 + 128] for d in range(4)]
        for b in range(4):
            shard = 4 * a + b
            dest = (shard % TX) * TA + shard // TX
            block = parts[0] if b == 0 else pltpu.roll(parts[0], (128 - 32 * b) % 128, 1)
            for d in range(1, 4):
                turned = parts[d] if d == b else pltpu.roll(parts[d], (32 * (d - b)) % 128, 1)
                block = jnp.where((lane >> 5) == d, turned, block)
            out_ref[dest, 0:16, :] = block
            out_ref[dest, 16:24, :] = tail_ref[...]


def first_kernel(activity_ref, prints_ref, places_ref, field_ref):
    field_ref[...] = jnp.zeros((FIELD, 128), F32)
    subtract_all(activity_ref, prints_ref, places_ref, field_ref)


def unpack_kernel(blocks_ref, partial_ref, movie_ref, field_ref):
    sub, lane = iotas()
    skew = (lane - 16 * sub) & 127
    turn = ((lane >> 4) - sub) & 7
    back = (lane + 16 * sub) & 127
    for r in range(CELL_ROWS):
        movie_ref[r * ROW : r * ROW + 8, :] = jnp.zeros((8, 128), F32)
        movie_ref[(r + 1) * ROW - 8 : (r + 1) * ROW, :] = jnp.zeros((8, 128), F32)

    def block(g, _):
        base = (1 + 8 * (g // TA)) * TA + g % TA
        for t in range(8):
            both = blocks_ref[g, 16 * t : 16 * t + 16, :].astype(F32)
            for h in range(2):
                value = both[8 * h : 8 * h + 8]
                value = pick_lanes(pick_rows(pick_lanes(value, skew), turn), back)
                movie_ref[pl.ds(base + (2 * t + h) * ROW, 8, stride=TA), :] = value
        return 0

    lax.fori_loop(0, GROUP, block, 0)
    field_ref[0:ROW, :] = partial_ref[0:ROW, :]
    field_ref[ROW + INNER :, :] = partial_ref[ROW + INNER :, :]

    def one(r, _):
        field_ref[pl.ds((r + 1) * ROW, ROW), :] = (
            partial_ref[pl.ds((r + 1) * ROW, ROW), :] + movie_ref[pl.ds(r * ROW, ROW), :]
        )
        return 0

    lax.fori_loop(0, CELL_ROWS, one, 0)


def update_kernel(field_ref, above_ref, below_ref, prints_ref, places_ref, out_ref, whole_ref):
    sub, lane = iotas()
    add_halo(field_ref, above_ref, below_ref, whole_ref)

    def leaf(v, m):
        folded = []
        for half in range(2):
            neuron = v * OWNED + (m // 4) * 8 + half * 4 + m % 4
            upper, lower = print_pair(prints_ref, neuron, sub, lane)
            top, bottom = patch(neuron, places_ref)
            value = upper * whole_ref[top, :] + lower * whole_ref[bottom, :]
            folded.append(value + pltpu.roll(value, 4, 0))
        return jnp.where(sub < 4, folded[0], folded[1])

    def tree(v, m, level):
        if level == 0:
            return leaf(v, m)
        shift = 1 << (level - 1)
        return merge_lanes(tree(v, m, level - 1), tree(v, m + shift, level - 1), shift, lane)

    def tile(v, _):
        total = tree(v, 0, 5)
        for g in range(GROUP):
            out_ref[g, pl.ds(pl.multiple_of(v * 8, 8), 8), :] = total
        return 0

    lax.fori_loop(0, TX, tile, 0)

    def squares(k, level):
        if level == 0:
            rows = prints_ref[pl.ds(k, 8, stride=OWNED), :]
            return rows * rows
        shift = 1 << (level - 1)
        return merge_lanes(squares(k, level - 1), squares(k + shift, level - 1), shift, lane)

    energy = squares(0, 6)
    energy = energy + pltpu.roll(energy, 64, 1)
    for g in range(GROUP):
        out_ref[g, 64:72, :] = energy


def trace_kernel(
    parts_ref, old_ref, movie_ref, prints_ref, places_ref, new_ref, weight_ref, field_ref
):
    sub, lane = iotas()
    start_field(movie_ref, field_ref)

    def total(start):
        rows = pl.ds(start, 8)
        value = parts_ref[0, rows, :]
        for g in range(1, GROUP):
            value = value + parts_ref[g, rows, :]
        return value

    energy = total(64)
    m = lane & 31
    own = (m >> 2) * 8 + (m & 3) + jnp.where(sub < 4, 0, 4)
    for v in range(TX):
        scale = pick_lanes(jnp.broadcast_to(energy[v : v + 1], (8, 128)), own)
        value = jnp.maximum(old_ref[v] + total(8 * v) / (scale + RIDGE), 0.0)
        new_ref[v] = value
        power = value * value
        power = power + pltpu.roll(power, 64, 1)
        power = power + pltpu.roll(power, 32, 1)
        power = merge_rows(power, power, 1, sub)
        power = merge_rows(power, power, 2, sub)
        weight_ref[v] = value / (power + RIDGE)
    subtract_all(new_ref, prints_ref, places_ref, field_ref)


def improve_prints(field_ref, above_ref, below_ref, weight_ref, prints_ref, places_ref, whole_ref, new_ref):
    sub, lane = iotas()
    add_halo(field_ref, above_ref, below_ref, whole_ref)

    def tile(v, _):
        value = weight_ref[v]

        def eight(q, _):
            base = pl.multiple_of(v * OWNED + q * 8, 8)
            folded = []
            for b in range(4):
                pair = spread(value, q * 4 + b, sub, lane)
                sides = []
                for half in range(2):
                    top, bottom = patch(base + half * 4 + b, places_ref)
                    sides.append(
                        merge_lanes(pair[half] * whole_ref[top, :], pair[half] * whole_ref[bottom, :], 64, lane)
                    )
                folded.append(merge_lanes(sides[0], sides[1], 32, lane))
            low = merge_rows(folded[0], folded[1], 1, sub)
            high = merge_rows(folded[2], folded[3], 1, sub)
            step = merge_rows(low, high, 2, sub)
            turned = pltpu.roll(step, 4, 0)
            dx = (lane & 32) != 0
            swapped = jnp.where(dx, pltpu.roll(turned, 32, 1), pltpu.roll(turned, 96, 1))
            step = jnp.where(dx == (sub >= 4), step, swapped)
            new_ref[pl.ds(base, 8), :] = jnp.maximum(prints_ref[pl.ds(base, 8), :] + step, 0.0)
            return 0

        return lax.fori_loop(0, 8, eight, 0)

    lax.fori_loop(0, TX, tile, 0)


def print_kernel(
    field_ref, above_ref, below_ref, weight_ref, activity_ref, movie_ref, prints_ref, places_ref,
    new_ref, next_ref, whole_ref,
):
    improve_prints(field_ref, above_ref, below_ref, weight_ref, prints_ref, places_ref, whole_ref, new_ref)
    start_field(movie_ref, next_ref)
    subtract_all(activity_ref, new_ref, places_ref, next_ref)


def last_kernel(
    field_ref, above_ref, below_ref, weight_ref, prints_ref, places_ref, out_ref, whole_ref, new_ref
):
    improve_prints(field_ref, above_ref, below_ref, weight_ref, prints_ref, places_ref, whole_ref, new_ref)
    for j in range(TX):
        rows = new_ref[j * OWNED : (j + 1) * OWNED, :]
        for z in range(TA):
            out_ref[j * TA + z] = rows


def finish_kernel(blocks_ref, out_ref):
    lane = lax.broadcasted_iota(jnp.int32, (OWNED, 128), 1)
    for z in range(TA):
        for a in range(2):
            parts = [blocks_ref[(4 * a + b) * TA + z] for b in range(4)]
            for d in range(4):
                row = parts[0] if d == 0 else pltpu.roll(parts[0], (128 - 32 * d) % 128, 1)
                for b in range(1, 4):
                    turned = parts[b] if b == d else pltpu.roll(parts[b], (32 * (b - d)) % 128, 1)
                    row = jnp.where((lane >> 5) == b, turned, row)
                start = d * 1024 + (z * 2 + a) * 128
                out_ref[:, start : start + 128] = row


def shape(*sizes, dtype=F32):
    return jax.ShapeDtypeStruct(sizes, dtype)


def call(kernel, outs, places, scratch=(), smem=None):
    return pl.pallas_call(
        kernel,
        out_shape=outs,
        in_specs=[SMEM if at == smem else VMEM for at in range(places)],
        out_specs=jax.tree.map(lambda _: VMEM, outs),
        scratch_shapes=list(scratch),
    )


FIELD_SHAPE = shape(FIELD, 128)
WHOLE = pltpu.VMEM((FIELD, 128), F32)
AXES = ("tx", "ta")


def exchange(blocks):
    return lax.all_to_all(blocks, AXES, 0, 0, tiled=True)


def halo(field):
    ends = lax.axis_size("ty") - 1
    above = lax.ppermute(field[INNER:], "ty", [(i, i + 1) for i in range(ends)])
    below = lax.ppermute(field[: 2 * ROW], "ty", [(i + 1, i) for i in range(ends)])
    return above, below


def shards(movie, footprints, traces, anchor_row, anchor_col):
    layer = lax.axis_index("ta")
    column = lax.axis_index("tx")
    frames = traces.shape[0]
    cells = movie.reshape(frames, 4, CELL_ROWS, TX, 2, 128).transpose(3, 1, 2, 0, 4, 5)
    movie_blocks = exchange(cells.reshape(GROUP, 128, 128))

    own = traces.reshape(frames, 8, 2, 4).transpose(2, 0, 1, 3).reshape(2, 128)
    anchors = jnp.concatenate([anchor_row, anchor_col]).astype(F32).reshape(1, 128)
    tail = jnp.concatenate([own, anchors, jnp.zeros((5, 128), F32)])
    rows = lax.dynamic_slice_in_dim(footprints, layer * 16, 16, axis=0)
    sent = call(pack_kernel, shape(GROUP, 24, 128), 2)(rows, tail)
    got = exchange(sent)
    prints = got[:, :16].reshape(COUNT, 128)
    activity = got[:, 16:18].reshape(TX, TA, 2, 128).transpose(0, 2, 1, 3).reshape(TX, 8, 128)
    spots = got.reshape(TX, TA, 24, 128)[:, 0, 18].astype(jnp.int32)
    tiles = jnp.arange(TX, dtype=jnp.int32)[:, None] * 8
    places = ((spots[:, :64] + 1) * ROW + (tiles + spots[:, 64:] + 1) * TA).reshape(COUNT)

    partial = call(first_kernel, FIELD_SHAPE, 3, smem=2)(activity, prints, places)
    cells, field = call(unpack_kernel, (shape(INNER, 128), FIELD_SHAPE), 2)(movie_blocks, partial)
    for sweep in range(ITERS):
        above, below = halo(field)
        sums = call(update_kernel, shape(GROUP, 72, 128), 5, (WHOLE,), smem=4)(
            field, above, below, prints, places
        )
        parts = exchange(sums)
        activity, weight, field = call(
            trace_kernel, (shape(TX, 8, 128), shape(TX, 8, 128), FIELD_SHAPE), 5, smem=4
        )(parts, activity, cells, prints, places)
        above, below = halo(field)
        if sweep + 1 < ITERS:
            prints, field = call(print_kernel, (shape(COUNT, 128), FIELD_SHAPE), 8, (WHOLE,), smem=7)(
                field, above, below, weight, activity, cells, prints, places
            )
        else:
            sent = call(
                last_kernel, shape(GROUP, OWNED, 128), 6, (WHOLE, pltpu.VMEM((COUNT, 128), F32)), smem=5
            )(field, above, below, weight, prints, places)
    footprints_out = call(finish_kernel, shape(OWNED, 4096), 1)(exchange(sent))
    mine = lax.dynamic_index_in_dim(activity, column, 0, keepdims=False).reshape(2, TA, 128)
    mine = lax.dynamic_index_in_dim(mine, layer, 1, keepdims=False)
    traces_out = mine.reshape(2, frames, 8, 4).transpose(1, 2, 0, 3).reshape(frames, OWNED)
    return footprints_out, traces_out


def solution(mesh):
    placed = (
        P("ta", None, "ty", "tx"),
        P(("ty", "tx"), None),
        P("ta", ("ty", "tx")),
        P(("ty", "tx")),
        P(("ty", "tx")),
    )
    return jax.shard_map(
        shards,
        mesh=mesh,
        in_specs=placed,
        out_specs=(P(("ty", "tx"), None), P("ta", ("ty", "tx"))),
        check_vma=False,
    )
```

```python
import functools

import jax
import jax.numpy as jnp
from jax import lax
from jax.experimental import pallas as pl
from jax.experimental.pallas import tpu as pltpu
from jax.sharding import PartitionSpec as P

ITERS = 2
RIDGE = 1.0
TX = 8
TA = 4
GROUP = TX * TA
OWNED = 64
COUNT = TX * OWNED
ROW = (TX * 8 + 2) * TA
CELL_ROWS = 16
FIELD = (CELL_ROWS + 2) * ROW
INNER = CELL_ROWS * ROW
VMEM = pl.BlockSpec(memory_space=pltpu.VMEM)
SMEM = pl.BlockSpec(memory_space=pltpu.SMEM)
F32 = jnp.float32


def iotas():
    return (
        lax.broadcasted_iota(jnp.int32, (8, 128), 0),
        lax.broadcasted_iota(jnp.int32, (8, 128), 1),
    )


def pick_lanes(value, index):
    return jnp.take_along_axis(value, index, axis=1, mode="promise_in_bounds")


def pick_rows(value, index):
    return jnp.take_along_axis(value, index, axis=0, mode="promise_in_bounds")


def merge_lanes(first, second, shift, lane):
    if shift == 64:
        high = lane >= 64
        return jnp.where(high, second, first) + pltpu.roll(jnp.where(high, first, second), 64, 1)
    return jnp.where(
        (lane & shift) != 0,
        second + pltpu.roll(second, shift, 1),
        first + pltpu.roll(first, 128 - shift, 1),
    )


def merge_rows(first, second, shift, sub):
    return jnp.where(
        (sub & shift) != 0,
        second + pltpu.roll(second, shift, 0),
        first + pltpu.roll(first, 8 - shift, 0),
    )


def spread(value, m, sub, lane):
    wide = pick_lanes(value, (lane & 96) + m)
    turned = pltpu.roll(wide, 4, 0)
    low = sub < 4
    return jnp.where(low, wide, turned), jnp.where(low, turned, wide)


def widen(prints, wide_ref):
    source = lax.broadcasted_iota(jnp.int32, (128, 512), 0)
    target = lax.broadcasted_iota(jnp.int32, (128, 512), 1)
    copies = (source == (target >> 7) * 32 + (target & 31)).astype(F32)
    wide = jnp.dot(prints, copies, precision=lax.Precision.HIGHEST, preferred_element_type=F32)
    for d in range(4):
        wide_ref[d] = wide[:, 128 * d : 128 * d + 128]


def print_pair(wide_ref, neuron, sub):
    rows = [jnp.broadcast_to(wide_ref[d, pl.ds(neuron, 1), :], (8, 128)) for d in range(4)]
    return jnp.where(sub < 4, rows[0], rows[1]), jnp.where(sub < 4, rows[2], rows[3])


def patch(v, k, places_ref):
    start = pl.multiple_of(places_ref[v, k], 4)
    return pl.ds(start, 8), pl.ds(start + ROW, 8)


def subtract_all(activity_ref, wide_ref, places_ref, field_ref):
    sub, lane = iotas()
    for first in range(2):
        tiles = [first + 2 * t for t in range(4)]
        values = [activity_ref[v] for v in tiles]

        def some(mh, _):
            for ml in range(4):
                pairs = [spread(value, mh * 4 + ml, sub, lane) for value in values]
                for half in range(2):
                    spots, changed = [], []
                    for v, pair in zip(tiles, pairs):
                        k = mh * 8 + half * 4 + ml
                        for at, side in zip(patch(v, k, places_ref), print_pair(wide_ref, v * OWNED + k, sub)):
                            spots.append(at)
                            changed.append(field_ref[at, :] - pair[half] * side)
                    for at, value in zip(spots, changed):
                        field_ref[at, :] = value
            return 0

        lax.fori_loop(0, 8, some, 0)


def start_field(movie_ref, field_ref):
    field_ref[0:ROW, :] = jnp.zeros((ROW, 128), F32)
    field_ref[ROW + INNER :, :] = jnp.zeros((ROW, 128), F32)

    def one(r, _):
        field_ref[pl.ds((r + 1) * ROW, ROW), :] = movie_ref[pl.ds(r * ROW, ROW), :]
        return 0

    lax.fori_loop(0, CELL_ROWS, one, 0)


def add_halo(field_ref, above_ref, below_ref):
    field_ref[0 : 2 * ROW, :] += above_ref[...]
    field_ref[INNER:, :] += below_ref[...]


def show_edges(field_ref, up_ref, down_ref):
    up_ref[...] = field_ref[0 : 2 * ROW, :]
    down_ref[...] = field_ref[INNER:, :]


def thirds(value):
    high = value.astype(jnp.bfloat16)
    rest = value - high.astype(F32)
    middle = rest.astype(jnp.bfloat16)
    return high, middle, (rest - middle.astype(F32)).astype(jnp.bfloat16)


def pack_kernel(cells_ref, prints_ref, traces_ref, row_ref, col_ref, layer_ref, out_ref):
    lane = lax.broadcasted_iota(jnp.int32, (16, 128), 1)
    rows = pl.ds(pl.multiple_of(layer_ref[0] * 16, 16), 16)
    tail = [piece.astype(F32) for piece in thirds(traces_ref[...])]
    tail = jnp.concatenate(tail + [row_ref[...].astype(F32), col_ref[...].astype(F32), jnp.zeros((2, OWNED), F32)], axis=0)
    tail = jnp.concatenate([tail, jnp.zeros((16, 128 - OWNED), F32)], axis=1).astype(jnp.bfloat16)
    for a in range(8):
        blocks = swap_lanes(
            [prints_ref[rows, d * 1024 + a * 128 : d * 1024 + a * 128 + 128] for d in range(4)], lane
        )
        for b in range(4):
            shard = 4 * a + b
            dest = (shard % TX) * TA + shard // TX
            out_ref[dest, 0:128, :] = cells_ref[dest]
            for at, piece in enumerate(thirds(blocks[b])):
                out_ref[dest, 128 + 16 * at : 144 + 16 * at, :] = piece
            out_ref[dest, 176:192, :] = tail


def unpack_kernel(got_ref, movie_ref, prints_ref, activity_ref, places_ref):
    sub, lane = iotas()
    skew = (lane - 16 * sub) & 127
    turn = ((lane >> 4) - sub) & 7
    back = (lane + 16 * sub) & 127
    for r in range(CELL_ROWS):
        movie_ref[r * ROW : r * ROW + 8, :] = jnp.zeros((8, 128), F32)
        movie_ref[(r + 1) * ROW - 8 : (r + 1) * ROW, :] = jnp.zeros((8, 128), F32)

    def block(g, _):
        base = (1 + 8 * (g // TA)) * TA + g % TA
        for t in range(8):
            both = got_ref[g, 16 * t : 16 * t + 16, :].astype(F32)
            for h in range(2):
                value = both[8 * h : 8 * h + 8]
                value = pick_lanes(pick_rows(pick_lanes(value, skew), turn), back)
                movie_ref[pl.ds(base + (2 * t + h) * ROW, 8, stride=TA), :] = value
        high, middle, low = [got_ref[g, 128 + 16 * at : 144 + 16 * at, :].astype(F32) for at in range(3)]
        prints_ref[pl.ds(pl.multiple_of(g * 16, 16), 16), :] = high + (middle + low)
        return 0

    lax.fori_loop(0, GROUP, block, 0)
    m = lane & 31
    own = (m >> 2) * 8 + (m & 3) + jnp.where(sub < 4, 0, 4)
    for v in range(TX):
        tails = [got_ref[v * TA + z, 176:192, :].astype(F32) for z in range(TA)]
        value = jnp.zeros((8, 128), F32)
        for f in range(4):
            rows = jnp.concatenate(
                [tail[f : f + 1] + (tail[4 + f : 5 + f] + tail[8 + f : 9 + f]) for tail in tails] * 2, axis=0
            )
            value = jnp.where((lane >> 5) == f, pick_lanes(rows, own), value)
        activity_ref[v] = value
        spots = (tails[0][12:13] + 1) * ROW + (tails[0][13:14] + (8 * v + 1)) * TA
        places_ref[v : v + 1, :] = spots.astype(jnp.int32)


def first_kernel(
    movie_ref, prints_ref, activity_ref, places_ref, wide_ref, field_ref, up_ref, down_ref
):
    widen(prints_ref[...], wide_ref)
    start_field(movie_ref, field_ref)
    subtract_all(activity_ref, wide_ref, places_ref, field_ref)
    show_edges(field_ref, up_ref, down_ref)


def update_kernel(old_ref, above_ref, below_ref, prints_ref, wide_ref, places_ref, out_ref, whole_ref):
    sub, lane = iotas()
    add_halo(whole_ref, above_ref, below_ref)

    def leaf(v, m):
        folded = []
        for half in range(2):
            k = (m // 4) * 8 + half * 4 + m % 4
            upper, lower = print_pair(wide_ref, v * OWNED + k, sub)
            top, bottom = patch(v, k, places_ref)
            value = upper * whole_ref[top, :] + lower * whole_ref[bottom, :]
            folded.append(value + pltpu.roll(value, 4, 0))
        return jnp.where(sub < 4, folded[0], folded[1])

    def tree(v, m, level):
        if level == 0:
            return leaf(v, m)
        shift = 1 << (level - 1)
        return merge_lanes(tree(v, m, level - 1), tree(v, m + shift, level - 1), shift, lane)

    def tile(v, _):
        total = tree(v, 0, 5)
        for g in range(GROUP):
            out_ref[g, pl.ds(pl.multiple_of(v * 8, 8), 8), :] = total
        return 0

    lax.fori_loop(0, TX, tile, 0)

    def squares(k, level):
        if level == 0:
            rows = prints_ref[pl.ds(k, 8, stride=OWNED), :]
            return rows * rows
        shift = 1 << (level - 1)
        return merge_lanes(squares(k, level - 1), squares(k + shift, level - 1), shift, lane)

    energy = squares(0, 6)
    energy = energy + pltpu.roll(energy, 64, 1)
    for g in range(GROUP):
        out_ref[g, 64:72, :] = energy


def trace_kernel(
    parts_ref, old_ref, movie_ref, wide_ref, places_ref, new_ref, weight_ref, field_ref, up_ref, down_ref
):
    sub, lane = iotas()
    start_field(movie_ref, field_ref)

    def total(start):
        rows = pl.ds(start, 8)
        value = parts_ref[0, rows, :]
        for g in range(1, GROUP):
            value = value + parts_ref[g, rows, :]
        return value

    energy = total(64)
    m = lane & 31
    own = (m >> 2) * 8 + (m & 3) + jnp.where(sub < 4, 0, 4)
    for v in range(TX):
        scale = pick_lanes(jnp.broadcast_to(energy[v : v + 1], (8, 128)), own)
        value = jnp.maximum(old_ref[v] + total(8 * v) / (scale + RIDGE), 0.0)
        new_ref[v] = value
        power = value * value
        power = power + pltpu.roll(power, 64, 1)
        power = power + pltpu.roll(power, 32, 1)
        power = merge_rows(power, power, 1, sub)
        power = merge_rows(power, power, 2, sub)
        weight_ref[v] = value / (power + RIDGE)
    subtract_all(new_ref, wide_ref, places_ref, field_ref)
    show_edges(field_ref, up_ref, down_ref)


def improve_prints(above_ref, below_ref, weight_ref, prints_ref, places_ref, whole_ref, new_ref):
    sub, lane = iotas()
    add_halo(whole_ref, above_ref, below_ref)

    def tile(v, _):
        value = weight_ref[v]

        def eight(q, _):
            base = pl.multiple_of(v * OWNED + q * 8, 8)
            folded = []
            for b in range(4):
                pair = spread(value, q * 4 + b, sub, lane)
                sides = []
                for half in range(2):
                    top, bottom = patch(v, q * 8 + half * 4 + b, places_ref)
                    sides.append(
                        merge_lanes(pair[half] * whole_ref[top, :], pair[half] * whole_ref[bottom, :], 64, lane)
                    )
                folded.append(merge_lanes(sides[0], sides[1], 32, lane))
            low = merge_rows(folded[0], folded[1], 1, sub)
            high = merge_rows(folded[2], folded[3], 1, sub)
            step = merge_rows(low, high, 2, sub)
            turned = pltpu.roll(step, 4, 0)
            dx = (lane & 32) != 0
            swapped = jnp.where(dx, pltpu.roll(turned, 32, 1), pltpu.roll(turned, 96, 1))
            step = jnp.where(dx == (sub >= 4), step, swapped)
            new_ref[pl.ds(base, 8), :] = jnp.maximum(prints_ref[pl.ds(base, 8), :] + step, 0.0)
            return 0

        return lax.fori_loop(0, 8, eight, 0, unroll=8)

    lax.fori_loop(0, TX, tile, 0)


def print_kernel(
    old_ref, above_ref, below_ref, weight_ref, activity_ref, movie_ref, prints_ref, places_ref,
    new_ref, wide_ref, next_ref, up_ref, down_ref, whole_ref,
):
    improve_prints(above_ref, below_ref, weight_ref, prints_ref, places_ref, whole_ref, new_ref)
    widen(new_ref[...], wide_ref)
    start_field(movie_ref, next_ref)
    subtract_all(activity_ref, wide_ref, places_ref, next_ref)
    show_edges(next_ref, up_ref, down_ref)


def last_kernel(
    old_ref, above_ref, below_ref, weight_ref, prints_ref, places_ref, out_ref, whole_ref, new_ref
):
    improve_prints(above_ref, below_ref, weight_ref, prints_ref, places_ref, whole_ref, new_ref)
    for j in range(TX):
        rows = new_ref[j * OWNED : (j + 1) * OWNED, :]
        for z in range(TA):
            out_ref[j * TA + z] = rows


def swap_lanes(parts, lane):
    for shift in (1, 2):
        high = (lane & (32 * shift)) != 0
        turned = []
        for b in range(4):
            other = pltpu.roll(parts[b ^ shift], 32 * shift if b & shift == 0 else 128 - 32 * shift, 1)
            turned.append(jnp.where(high, other, parts[b]) if b & shift == 0 else jnp.where(high, parts[b], other))
        parts = turned
    return parts


def finish_kernel(blocks_ref, out_ref):
    lane = lax.broadcasted_iota(jnp.int32, (OWNED, 128), 1)
    for z in range(TA):
        for a in range(2):
            rows = swap_lanes([blocks_ref[(4 * a + b) * TA + z] for b in range(4)], lane)
            for d in range(4):
                start = d * 1024 + (z * 2 + a) * 128
                out_ref[:, start : start + 128] = rows[d]


def shape(*sizes, dtype=F32):
    return jax.ShapeDtypeStruct(sizes, dtype)


def call(kernel, outs, places, scratch=(), smem=None, alias=None):
    return pl.pallas_call(
        kernel,
        out_shape=outs,
        in_specs=[SMEM if at == smem else VMEM for at in range(places)],
        out_specs=jax.tree.map(lambda _: VMEM, outs),
        scratch_shapes=list(scratch),
        input_output_aliases={} if alias is None else {0: alias},
        compiler_params=pltpu.CompilerParams(vmem_limit_bytes=16 << 20),
    )


FIELD_SHAPE = shape(FIELD, 128)
EDGE_SHAPE = shape(2 * ROW, 128)
WIDE_SHAPE = shape(4, COUNT, 128)
AXES = ("tx", "ta")


def exchange(blocks):
    return lax.all_to_all(blocks, AXES, 0, 0, tiled=True)


def halo(up, down):
    ends = lax.axis_size("ty") - 1
    above = lax.ppermute(down, "ty", [(i, i + 1) for i in range(ends)])
    below = lax.ppermute(up, "ty", [(i + 1, i) for i in range(ends)])
    return above, below


def shards(movie, footprints, traces, anchor_row, anchor_col):
    layer = lax.axis_index("ta")
    column = lax.axis_index("tx")
    frames = traces.shape[0]
    blocks = movie.reshape(frames, 4, CELL_ROWS, TX, 2, 128).transpose(3, 1, 2, 0, 4, 5)
    got = exchange(
        call(pack_kernel, shape(GROUP, 192, 128, dtype=jnp.bfloat16), 6, smem=5)(
            blocks.reshape(GROUP, 128, 128),
            footprints,
            traces,
            anchor_row.reshape(1, OWNED),
            anchor_col.reshape(1, OWNED),
            layer.reshape(1),
        )
    )
    cells, prints, activity, places = call(
        unpack_kernel,
        (shape(INNER, 128), shape(COUNT, 128), shape(TX, 8, 128), shape(TX, 128, dtype=jnp.int32)),
        1,
    )(got)
    wide, field, up, down = call(
        first_kernel, (WIDE_SHAPE, FIELD_SHAPE, EDGE_SHAPE, EDGE_SHAPE), 4, smem=3
    )(cells, prints, activity, places)
    for sweep in range(ITERS):
        above, below = halo(up, down)
        sums, _ = call(update_kernel, (shape(GROUP, 72, 128), FIELD_SHAPE), 6, smem=5, alias=1)(
            field, above, below, prints, wide, places
        )
        parts = exchange(sums)
        activity, weight, field, up, down = call(
            trace_kernel,
            (shape(TX, 8, 128), shape(TX, 8, 128), FIELD_SHAPE, EDGE_SHAPE, EDGE_SHAPE),
            5,
            smem=4,
        )(parts, activity, cells, wide, places)
        above, below = halo(up, down)
        if sweep + 1 < ITERS:
            prints, wide, field, up, down, _ = call(
                print_kernel,
                (shape(COUNT, 128), WIDE_SHAPE, FIELD_SHAPE, EDGE_SHAPE, EDGE_SHAPE, FIELD_SHAPE),
                8,
                smem=7,
                alias=5,
            )(field, above, below, weight, activity, cells, prints, places)
        else:
            sent, _ = call(
                last_kernel,
                (shape(GROUP, OWNED, 128), FIELD_SHAPE),
                6,
                (pltpu.VMEM((COUNT, 128), F32),),
                smem=5,
                alias=1,
            )(field, above, below, weight, prints, places)
    footprints_out = call(finish_kernel, shape(OWNED, 4096), 1)(exchange(sent))
    mine = lax.dynamic_index_in_dim(activity, column, 0, keepdims=False).reshape(2, TA, 128)
    mine = lax.dynamic_index_in_dim(mine, layer, 1, keepdims=False)
    traces_out = mine.reshape(2, frames, 8, 4).transpose(1, 2, 0, 3).reshape(frames, OWNED)
    return footprints_out, traces_out


def solution(mesh):
    placed = (
        P("ta", None, "ty", "tx"),
        P(("ty", "tx"), None),
        P("ta", ("ty", "tx")),
        P(("ty", "tx")),
        P(("ty", "tx")),
    )
    return jax.shard_map(
        shards,
        mesh=mesh,
        in_specs=placed,
        out_specs=(P(("ty", "tx"), None), P("ta", ("ty", "tx"))),
        check_vma=False,
    )
```

```python
import functools

import jax
import jax.numpy as jnp
from jax import lax
from jax.experimental import pallas as pl
from jax.experimental.pallas import tpu as pltpu
from jax.sharding import PartitionSpec as P

ITERS = 2
RIDGE = 1.0
TX = 8
TA = 4
GROUP = TX * TA
OWNED = 64
COUNT = TX * OWNED
ROW = (TX * 8 + 2) * TA
CELL_ROWS = 16
FIELD = (CELL_ROWS + 2) * ROW
INNER = CELL_ROWS * ROW
VMEM = pl.BlockSpec(memory_space=pltpu.VMEM)
SMEM = pl.BlockSpec(memory_space=pltpu.SMEM)
F32 = jnp.float32


def iotas():
    return (
        lax.broadcasted_iota(jnp.int32, (8, 128), 0),
        lax.broadcasted_iota(jnp.int32, (8, 128), 1),
    )


def pick_lanes(value, index):
    return jnp.take_along_axis(value, index, axis=1, mode="promise_in_bounds")


def pick_rows(value, index):
    return jnp.take_along_axis(value, index, axis=0, mode="promise_in_bounds")


def merge_lanes(first, second, shift, lane):
    if shift == 64:
        high = lane >= 64
        return jnp.where(high, second, first) + pltpu.roll(jnp.where(high, first, second), 64, 1)
    return jnp.where(
        (lane & shift) != 0,
        second + pltpu.roll(second, shift, 1),
        first + pltpu.roll(first, 128 - shift, 1),
    )


def merge_rows(first, second, shift, sub):
    return jnp.where(
        (sub & shift) != 0,
        second + pltpu.roll(second, shift, 0),
        first + pltpu.roll(first, 8 - shift, 0),
    )


def spread(value, m, sub, lane):
    wide = pick_lanes(value, (lane & 96) + m)
    turned = pltpu.roll(wide, 4, 0)
    low = sub < 4
    return jnp.where(low, wide, turned), jnp.where(low, turned, wide)


def widen(prints, wide_ref):
    source = lax.broadcasted_iota(jnp.int32, (128, 512), 0)
    target = lax.broadcasted_iota(jnp.int32, (128, 512), 1)
    copies = (source == (target >> 7) * 32 + (target & 31)).astype(F32)
    wide = jnp.dot(prints, copies, precision=lax.Precision.HIGHEST, preferred_element_type=F32)
    for d in range(4):
        wide_ref[d] = wide[:, 128 * d : 128 * d + 128]


def print_pair(wide_ref, neuron, sub):
    rows = [jnp.broadcast_to(wide_ref[d, pl.ds(neuron, 1), :], (8, 128)) for d in range(4)]
    return jnp.where(sub < 4, rows[0], rows[1]), jnp.where(sub < 4, rows[2], rows[3])


def patch(v, k, places_ref):
    start = pl.multiple_of(places_ref[v, k], 4)
    return pl.ds(start, 8), pl.ds(start + ROW, 8)


def subtract_all(activity_ref, wide_ref, places_ref, field_ref):
    sub, lane = iotas()
    for first in range(2):
        tiles = [first + 2 * t for t in range(4)]
        values = [activity_ref[v] for v in tiles]

        def some(mh, _):
            for ml in range(4):
                pairs = [spread(value, mh * 4 + ml, sub, lane) for value in values]
                for half in range(2):
                    spots, changed = [], []
                    for v, pair in zip(tiles, pairs):
                        k = mh * 8 + half * 4 + ml
                        for at, side in zip(patch(v, k, places_ref), print_pair(wide_ref, v * OWNED + k, sub)):
                            spots.append(at)
                            changed.append(field_ref[at, :] - pair[half] * side)
                    for at, value in zip(spots, changed):
                        field_ref[at, :] = value
            return 0

        lax.fori_loop(0, 8, some, 0)


def start_field(movie_ref, field_ref):
    field_ref[0:ROW, :] = jnp.zeros((ROW, 128), F32)
    field_ref[ROW + INNER :, :] = jnp.zeros((ROW, 128), F32)

    def one(r, _):
        field_ref[pl.ds((r + 1) * ROW, ROW), :] = movie_ref[pl.ds(r * ROW, ROW), :]
        return 0

    lax.fori_loop(0, CELL_ROWS, one, 0)


def add_halo(field_ref, above_ref, below_ref, near_ref):
    even = near_ref[0] == 0
    top = jnp.where(even, below_ref[...], above_ref[...])
    bottom = jnp.where(even, above_ref[...], below_ref[...])
    field_ref[0 : 2 * ROW, :] += top
    field_ref[INNER:, :] += bottom


def show_edges(field_ref, near_ref, near_out, far_out):
    even = near_ref[0] == 0
    top = field_ref[0 : 2 * ROW, :]
    bottom = field_ref[INNER:, :]
    near_out[...] = jnp.where(even, bottom, top)
    far_out[...] = jnp.where(even, top, bottom)


def pieces(value, count):
    out = []
    for _ in range(count):
        out.append(value.astype(jnp.bfloat16))
        value = value - out[-1].astype(F32)
    return out


def pack_kernel(cells_ref, prints_ref, small_ref, layer_ref, out_ref):
    lane = lax.broadcasted_iota(jnp.int32, (16, 128), 1)
    rows = pl.ds(pl.multiple_of(layer_ref[0] * 16, 16), 16)
    tail = [piece.astype(F32) for piece in pieces(small_ref[0:2, :], 3)]
    tail = jnp.concatenate(tail + [small_ref[2:3, :], jnp.zeros((9, 128), F32)], axis=0).astype(jnp.bfloat16)
    for a in range(8):
        blocks = swap_lanes(
            [prints_ref[rows, d * 1024 + a * 128 : d * 1024 + a * 128 + 128] for d in range(4)], lane
        )
        for b in range(4):
            shard = 4 * a + b
            dest = (shard % TX) * TA + shard // TX
            out_ref[dest, 0:128, :] = cells_ref[dest]
            for at, piece in enumerate(pieces(blocks[b], 2)):
                out_ref[dest, 128 + 16 * at : 144 + 16 * at, :] = piece
            out_ref[dest, 160:168, :] = tail[0:8]


def unpack_kernel(got_ref, movie_ref, prints_ref, activity_ref, places_ref):
    sub, lane = iotas()
    skew = (lane - 16 * sub) & 127
    turn = ((lane >> 4) - sub) & 7
    back = (lane + 16 * sub) & 127
    for r in range(CELL_ROWS):
        movie_ref[r * ROW : r * ROW + 8, :] = jnp.zeros((8, 128), F32)
        movie_ref[(r + 1) * ROW - 8 : (r + 1) * ROW, :] = jnp.zeros((8, 128), F32)

    def block(g, _):
        base = (1 + 8 * (g // TA)) * TA + g % TA
        for t in range(8):
            both = got_ref[g, 16 * t : 16 * t + 16, :].astype(F32)
            for h in range(2):
                value = both[8 * h : 8 * h + 8]
                value = pick_lanes(pick_rows(pick_lanes(value, skew), turn), back)
                movie_ref[pl.ds(base + (2 * t + h) * ROW, 8, stride=TA), :] = value
        high, low = [got_ref[g, 128 + 16 * at : 144 + 16 * at, :].astype(F32) for at in range(2)]
        prints_ref[pl.ds(pl.multiple_of(g * 16, 16), 16), :] = high + low
        return 0

    lax.fori_loop(0, GROUP, block, 0, unroll=2)
    for v in range(TX):
        tails = [got_ref[v * TA + z, 160:168, :].astype(F32) for z in range(TA)]
        values = [tail[0:2] + (tail[2:4] + tail[4:6]) for tail in tails]
        activity_ref[v] = jnp.concatenate([value[h : h + 1] for h in range(2) for value in values], axis=0)
        row, col = tails[0][6:7], pltpu.roll(tails[0], 64, 1)[6:7]
        places_ref[v : v + 1, :] = ((row + 1) * ROW + (col + (8 * v + 1)) * TA).astype(jnp.int32)


def first_kernel(
    movie_ref, prints_ref, activity_ref, near_ref, places_ref, wide_ref, field_ref, up_ref, down_ref
):
    widen(prints_ref[...], wide_ref)
    start_field(movie_ref, field_ref)
    subtract_all(activity_ref, wide_ref, places_ref, field_ref)
    show_edges(field_ref, near_ref, up_ref, down_ref)


def update_kernel(old_ref, above_ref, below_ref, prints_ref, wide_ref, near_ref, places_ref, out_ref, whole_ref):
    sub, lane = iotas()
    add_halo(whole_ref, above_ref, below_ref, near_ref)

    def leaf(v, m):
        folded = []
        for half in range(2):
            k = (m // 4) * 8 + half * 4 + m % 4
            upper, lower = print_pair(wide_ref, v * OWNED + k, sub)
            top, bottom = patch(v, k, places_ref)
            value = upper * whole_ref[top, :] + lower * whole_ref[bottom, :]
            folded.append(value + pltpu.roll(value, 4, 0))
        return jnp.where(sub < 4, folded[0], folded[1])

    def tree(v, m, level):
        if level == 0:
            return leaf(v, m)
        shift = 1 << (level - 1)
        return merge_lanes(tree(v, m, level - 1), tree(v, m + shift, level - 1), shift, lane)

    def tile(v, _):
        total = tree(v, 0, 5)
        for g in range(GROUP):
            out_ref[g, pl.ds(pl.multiple_of(v * 8, 8), 8), :] = total
        return 0

    lax.fori_loop(0, TX, tile, 0)

    def squares(k, level):
        if level == 0:
            rows = prints_ref[pl.ds(k, 8, stride=OWNED), :]
            return rows * rows
        shift = 1 << (level - 1)
        return merge_lanes(squares(k, level - 1), squares(k + shift, level - 1), shift, lane)

    energy = squares(0, 6)
    energy = energy + pltpu.roll(energy, 64, 1)
    for g in range(GROUP):
        out_ref[g, 64:72, :] = energy


def trace_kernel(
    parts_ref, old_ref, movie_ref, wide_ref, near_ref, places_ref, new_ref, weight_ref, field_ref, up_ref, down_ref
):
    sub, lane = iotas()
    start_field(movie_ref, field_ref)

    def total(start):
        rows = pl.ds(start, 8)
        value = parts_ref[0, rows, :]
        for g in range(1, GROUP):
            value = value + parts_ref[g, rows, :]
        return value

    energy = total(64)
    m = lane & 31
    own = (m >> 2) * 8 + (m & 3) + jnp.where(sub < 4, 0, 4)
    for v in range(TX):
        scale = pick_lanes(jnp.broadcast_to(energy[v : v + 1], (8, 128)), own)
        value = jnp.maximum(old_ref[v] + total(8 * v) / (scale + RIDGE), 0.0)
        new_ref[v] = value
        power = value * value
        power = power + pltpu.roll(power, 64, 1)
        power = power + pltpu.roll(power, 32, 1)
        power = merge_rows(power, power, 1, sub)
        power = merge_rows(power, power, 2, sub)
        weight_ref[v] = value / (power + RIDGE)
    subtract_all(new_ref, wide_ref, places_ref, field_ref)
    show_edges(field_ref, near_ref, up_ref, down_ref)


def improve_prints(above_ref, below_ref, weight_ref, prints_ref, near_ref, places_ref, whole_ref, new_ref):
    sub, lane = iotas()
    add_halo(whole_ref, above_ref, below_ref, near_ref)

    def tile(v, _):
        value = weight_ref[v]

        def eight(q, _):
            base = pl.multiple_of(v * OWNED + q * 8, 8)
            folded = []
            for b in range(4):
                pair = spread(value, q * 4 + b, sub, lane)
                sides = []
                for half in range(2):
                    top, bottom = patch(v, q * 8 + half * 4 + b, places_ref)
                    sides.append(
                        merge_lanes(pair[half] * whole_ref[top, :], pair[half] * whole_ref[bottom, :], 64, lane)
                    )
                folded.append(merge_lanes(sides[0], sides[1], 32, lane))
            low = merge_rows(folded[0], folded[1], 1, sub)
            high = merge_rows(folded[2], folded[3], 1, sub)
            step = merge_rows(low, high, 2, sub)
            turned = pltpu.roll(step, 4, 0)
            dx = (lane & 32) != 0
            swapped = jnp.where(dx, pltpu.roll(turned, 32, 1), pltpu.roll(turned, 96, 1))
            step = jnp.where(dx == (sub >= 4), step, swapped)
            new_ref[pl.ds(base, 8), :] = jnp.maximum(prints_ref[pl.ds(base, 8), :] + step, 0.0)
            return 0

        return lax.fori_loop(0, 8, eight, 0, unroll=8)

    lax.fori_loop(0, TX, tile, 0)


def print_kernel(
    old_ref, above_ref, below_ref, weight_ref, activity_ref, movie_ref, prints_ref, near_ref, places_ref,
    new_ref, wide_ref, next_ref, up_ref, down_ref, whole_ref,
):
    improve_prints(above_ref, below_ref, weight_ref, prints_ref, near_ref, places_ref, whole_ref, new_ref)
    widen(new_ref[...], wide_ref)
    start_field(movie_ref, next_ref)
    subtract_all(activity_ref, wide_ref, places_ref, next_ref)
    show_edges(next_ref, near_ref, up_ref, down_ref)


def last_kernel(
    old_ref, above_ref, below_ref, weight_ref, prints_ref, near_ref, places_ref, out_ref, whole_ref, new_ref
):
    improve_prints(above_ref, below_ref, weight_ref, prints_ref, near_ref, places_ref, whole_ref, new_ref)
    for j in range(TX):
        rows = new_ref[j * OWNED : (j + 1) * OWNED, :]
        for z in range(TA):
            out_ref[j * TA + z] = rows


def swap_lanes(parts, lane):
    for shift in (1, 2):
        high = (lane & (32 * shift)) != 0
        turned = []
        for b in range(4):
            other = pltpu.roll(parts[b ^ shift], 32 * shift if b & shift == 0 else 128 - 32 * shift, 1)
            turned.append(jnp.where(high, other, parts[b]) if b & shift == 0 else jnp.where(high, parts[b], other))
        parts = turned
    return parts


def finish_kernel(blocks_ref, out_ref):
    lane = lax.broadcasted_iota(jnp.int32, (OWNED, 128), 1)
    for z in range(TA):
        for a in range(2):
            rows = swap_lanes([blocks_ref[(4 * a + b) * TA + z] for b in range(4)], lane)
            for d in range(4):
                start = d * 1024 + (z * 2 + a) * 128
                out_ref[:, start : start + 128] = rows[d]


def shape(*sizes, dtype=F32):
    return jax.ShapeDtypeStruct(sizes, dtype)


def call(kernel, outs, places, scratch=(), smem=(), alias=None):
    return pl.pallas_call(
        kernel,
        out_shape=outs,
        in_specs=[SMEM if at in smem else VMEM for at in range(places)],
        out_specs=jax.tree.map(lambda _: VMEM, outs),
        scratch_shapes=list(scratch),
        input_output_aliases={} if alias is None else {0: alias},
        compiler_params=pltpu.CompilerParams(vmem_limit_bytes=16 << 20),
    )


FIELD_SHAPE = shape(FIELD, 128)
EDGE_SHAPE = shape(2 * ROW, 128)
WIDE_SHAPE = shape(4, COUNT, 128)
AXES = ("tx", "ta")


def exchange(blocks):
    return lax.all_to_all(blocks, AXES, 0, 0, tiled=True)


def halo(near, far):
    near = lax.ppermute(near, "ty", [(0, 1), (1, 0), (2, 3), (3, 2)])
    return near, lax.ppermute(far, "ty", [(1, 2), (2, 1)])


def shards(movie, footprints, traces, anchor_row, anchor_col):
    layer = lax.axis_index("ta")
    column = lax.axis_index("tx")
    frames = traces.shape[0]
    index = lax.axis_index("ty")
    near = (index % 2).reshape(1)
    blocks = movie.reshape(frames, 4, CELL_ROWS, TX, 2, 128).transpose(3, 1, 2, 0, 4, 5)
    own = traces.reshape(frames, 8, 2, 4).transpose(2, 0, 1, 3).reshape(2, 128)
    spots = jnp.concatenate([anchor_row, anchor_col]).astype(F32).reshape(1, 128)
    got = exchange(
        call(pack_kernel, shape(GROUP, 168, 128, dtype=jnp.bfloat16), 4, smem=(3,))(
            blocks.reshape(GROUP, 128, 128), footprints, jnp.concatenate([own, spots]), layer.reshape(1)
        )
    )
    cells, prints, activity, places = call(
        unpack_kernel,
        (shape(INNER, 128), shape(COUNT, 128), shape(TX, 8, 128), shape(TX, 128, dtype=jnp.int32)),
        1,
    )(got)
    wide, field, up, down = call(
        first_kernel, (WIDE_SHAPE, FIELD_SHAPE, EDGE_SHAPE, EDGE_SHAPE), 5, smem=(3, 4)
    )(cells, prints, activity, near, places)
    for sweep in range(ITERS):
        above, below = halo(up, down)
        sums, _ = call(update_kernel, (shape(GROUP, 72, 128), FIELD_SHAPE), 7, smem=(5, 6), alias=1)(
            field, above, below, prints, wide, near, places
        )
        parts = exchange(sums)
        activity, weight, field, up, down = call(
            trace_kernel,
            (shape(TX, 8, 128), shape(TX, 8, 128), FIELD_SHAPE, EDGE_SHAPE, EDGE_SHAPE),
            6,
            smem=(4, 5),
        )(parts, activity, cells, wide, near, places)
        above, below = halo(up, down)
        if sweep + 1 < ITERS:
            prints, wide, field, up, down, _ = call(
                print_kernel,
                (shape(COUNT, 128), WIDE_SHAPE, FIELD_SHAPE, EDGE_SHAPE, EDGE_SHAPE, FIELD_SHAPE),
                9,
                smem=(7, 8),
                alias=5,
            )(field, above, below, weight, activity, cells, prints, near, places)
        else:
            sent, _ = call(
                last_kernel,
                (shape(GROUP, OWNED, 128), FIELD_SHAPE),
                7,
                (pltpu.VMEM((COUNT, 128), F32),),
                smem=(5, 6),
                alias=1,
            )(field, above, below, weight, prints, near, places)
    footprints_out = call(finish_kernel, shape(OWNED, 4096), 1)(exchange(sent))
    mine = lax.dynamic_index_in_dim(activity, column, 0, keepdims=False).reshape(2, TA, 128)
    mine = lax.dynamic_index_in_dim(mine, layer, 1, keepdims=False)
    traces_out = mine.reshape(2, frames, 8, 4).transpose(1, 2, 0, 3).reshape(frames, OWNED)
    return footprints_out, traces_out


def solution(mesh):
    placed = (
        P("ta", None, "ty", "tx"),
        P(("ty", "tx"), None),
        P("ta", ("ty", "tx")),
        P(("ty", "tx")),
        P(("ty", "tx")),
    )
    return jax.shard_map(
        shards,
        mesh=mesh,
        in_specs=placed,
        out_specs=(P(("ty", "tx"), None), P("ta", ("ty", "tx"))),
        check_vma=False,
    )
```

```python
import functools

import jax
import jax.numpy as jnp
from jax import lax
from jax.experimental import pallas as pl
from jax.experimental.pallas import tpu as pltpu
from jax.sharding import PartitionSpec as P

ITERS = 2
RIDGE = 1.0
TX = 8
TA = 4
GROUP = TX * TA
OWNED = 64
COUNT = TX * OWNED
ROW = (TX * 8 + 2) * TA
CELL_ROWS = 16
FIELD = (CELL_ROWS + 2) * ROW
INNER = CELL_ROWS * ROW
VMEM = pl.BlockSpec(memory_space=pltpu.VMEM)
SMEM = pl.BlockSpec(memory_space=pltpu.SMEM)
ANY = pl.BlockSpec(memory_space=pl.ANY)
F32 = jnp.float32


def iotas():
    return (
        lax.broadcasted_iota(jnp.int32, (8, 128), 0),
        lax.broadcasted_iota(jnp.int32, (8, 128), 1),
    )


def pick_lanes(value, index):
    return jnp.take_along_axis(value, index, axis=1, mode="promise_in_bounds")


def pick_rows(value, index):
    return jnp.take_along_axis(value, index, axis=0, mode="promise_in_bounds")


def merge_lanes(first, second, shift, lane):
    if shift == 64:
        high = lane >= 64
        return jnp.where(high, second, first) + pltpu.roll(jnp.where(high, first, second), 64, 1)
    return jnp.where(
        (lane & shift) != 0,
        second + pltpu.roll(second, shift, 1),
        first + pltpu.roll(first, 128 - shift, 1),
    )


def merge_rows(first, second, shift, sub):
    return jnp.where(
        (sub & shift) != 0,
        second + pltpu.roll(second, shift, 0),
        first + pltpu.roll(first, 8 - shift, 0),
    )


def spread(value, m, sub, lane):
    wide = pick_lanes(value, (lane & 96) + m)
    turned = pltpu.roll(wide, 4, 0)
    low = sub < 4
    return jnp.where(low, wide, turned), jnp.where(low, turned, wide)


def pieces(value, count):
    out = []
    for _ in range(count):
        out.append(value.astype(jnp.bfloat16))
        value = value - out[-1].astype(F32)
    return out


def widen(prints, wide_ref):
    source = lax.broadcasted_iota(jnp.int32, (384, 512), 0) & 127
    target = lax.broadcasted_iota(jnp.int32, (384, 512), 1)
    copies = (source == (target >> 7) * 32 + (target & 31)).astype(jnp.bfloat16)
    parts = jnp.concatenate(pieces(prints, 3), axis=1)
    wide = jnp.dot(parts, copies, preferred_element_type=F32)
    for d in range(4):
        wide_ref[d] = wide[:, 128 * d : 128 * d + 128]


def print_pair(wide_ref, neuron, sub):
    rows = [jnp.broadcast_to(wide_ref[d, pl.ds(neuron, 1), :], (8, 128)) for d in range(4)]
    return jnp.where(sub < 4, rows[0], rows[1]), jnp.where(sub < 4, rows[2], rows[3])


def patch(v, k, places_ref):
    start = pl.multiple_of(places_ref[v, k], 4)
    return pl.ds(start, 8), pl.ds(start + ROW, 8)


def subtract_all(activity_ref, wide_ref, places_ref, field_ref):
    sub, lane = iotas()
    for first in range(2):
        tiles = [first + 2 * t for t in range(4)]
        values = [activity_ref[v] for v in tiles]

        def some(mh, _):
            for ml in range(4):
                pairs = [spread(value, mh * 4 + ml, sub, lane) for value in values]
                for half in range(2):
                    spots, changed = [], []
                    for v, pair in zip(tiles, pairs):
                        k = mh * 8 + half * 4 + ml
                        for at, side in zip(patch(v, k, places_ref), print_pair(wide_ref, v * OWNED + k, sub)):
                            spots.append(at)
                            changed.append(field_ref[at, :] - pair[half] * side)
                    for at, value in zip(spots, changed):
                        field_ref[at, :] = value
            return 0

        lax.fori_loop(0, 8, some, 0)


def start_field(movie_ref, field_ref):
    field_ref[0:ROW, :] = jnp.zeros((ROW, 128), F32)
    field_ref[ROW + INNER :, :] = jnp.zeros((ROW, 128), F32)

    def one(r, _):
        field_ref[pl.ds((r + 1) * ROW, ROW), :] = movie_ref[pl.ds(r * ROW, ROW), :]
        return 0

    lax.fori_loop(0, CELL_ROWS, one, 0)


def add_halo(field_ref, above_ref, below_ref, near_ref):
    even = near_ref[0] == 0
    top = jnp.where(even, below_ref[...], above_ref[...])
    bottom = jnp.where(even, above_ref[...], below_ref[...])
    field_ref[0 : 2 * ROW, :] += top
    field_ref[INNER:, :] += bottom


def show_edges(field_ref, near_ref, near_out, far_out):
    even = near_ref[0] == 0
    top = field_ref[0 : 2 * ROW, :]
    bottom = field_ref[INNER:, :]
    near_out[...] = jnp.where(even, bottom, top)
    far_out[...] = jnp.where(even, top, bottom)


def pack_kernel(cells_ref, prints_ref, small_ref, layer_ref, out_ref):
    lane = lax.broadcasted_iota(jnp.int32, (16, 128), 1)
    rows = pl.ds(pl.multiple_of(layer_ref[0] * 16, 16), 16)
    tail = [piece.astype(F32) for piece in pieces(small_ref[0:2, :], 3)]
    tail = jnp.concatenate(tail + [small_ref[2:3, :], jnp.zeros((9, 128), F32)], axis=0).astype(jnp.bfloat16)
    for a in range(8):
        blocks = swap_lanes(
            [prints_ref[rows, d * 1024 + a * 128 : d * 1024 + a * 128 + 128] for d in range(4)], lane
        )
        for b in range(4):
            shard = 4 * a + b
            dest = (shard % TX) * TA + shard // TX
            out_ref[dest, 0:128, :] = cells_ref[dest]
            for at, piece in enumerate(pieces(blocks[b], 2)):
                out_ref[dest, 128 + 16 * at : 144 + 16 * at, :] = piece
            out_ref[dest, 160:168, :] = tail[0:8]


def unpack_kernel(got_ref, movie_ref, prints_ref, activity_ref, places_ref):
    sub, lane = iotas()
    skew = (lane - 16 * sub) & 127
    turn = ((lane >> 4) - sub) & 7
    back = (lane + 16 * sub) & 127
    for r in range(CELL_ROWS):
        movie_ref[r * ROW : r * ROW + 8, :] = jnp.zeros((8, 128), F32)
        movie_ref[(r + 1) * ROW - 8 : (r + 1) * ROW, :] = jnp.zeros((8, 128), F32)

    def block(g, _):
        base = (1 + 8 * (g // TA)) * TA + g % TA
        for t in range(8):
            both = got_ref[g, 16 * t : 16 * t + 16, :].astype(F32)
            for h in range(2):
                value = both[8 * h : 8 * h + 8]
                value = pick_lanes(pick_rows(pick_lanes(value, skew), turn), back)
                movie_ref[pl.ds(base + (2 * t + h) * ROW, 8, stride=TA), :] = value
        high, low = [got_ref[g, 128 + 16 * at : 144 + 16 * at, :].astype(F32) for at in range(2)]
        prints_ref[pl.ds(pl.multiple_of(g * 16, 16), 16), :] = high + low
        return 0

    lax.fori_loop(0, GROUP, block, 0, unroll=2)
    for v in range(TX):
        tails = [got_ref[v * TA + z, 160:168, :].astype(F32) for z in range(TA)]
        values = [tail[0:2] + (tail[2:4] + tail[4:6]) for tail in tails]
        activity_ref[v] = jnp.concatenate([value[h : h + 1] for h in range(2) for value in values], axis=0)
        row, col = tails[0][6:7], pltpu.roll(tails[0], 64, 1)[6:7]
        places_ref[v : v + 1, :] = ((row + 1) * ROW + (col + (8 * v + 1)) * TA).astype(jnp.int32)


def first_kernel(
    movie_ref, prints_ref, activity_ref, near_ref, places_ref, wide_ref, field_ref, up_ref, down_ref
):
    widen(prints_ref[...], wide_ref)
    start_field(movie_ref, field_ref)
    subtract_all(activity_ref, wide_ref, places_ref, field_ref)
    show_edges(field_ref, near_ref, up_ref, down_ref)


def update_kernel(old_ref, above_ref, below_ref, prints_ref, wide_ref, near_ref, places_ref, out_ref, whole_ref):
    sub, lane = iotas()
    add_halo(whole_ref, above_ref, below_ref, near_ref)

    def leaf(v, m):
        folded = []
        for half in range(2):
            k = (m // 4) * 8 + half * 4 + m % 4
            upper, lower = print_pair(wide_ref, v * OWNED + k, sub)
            top, bottom = patch(v, k, places_ref)
            value = upper * whole_ref[top, :] + lower * whole_ref[bottom, :]
            folded.append(value + pltpu.roll(value, 4, 0))
        return jnp.where(sub < 4, folded[0], folded[1])

    def tree(v, m, level):
        if level == 0:
            return leaf(v, m)
        shift = 1 << (level - 1)
        return merge_lanes(tree(v, m, level - 1), tree(v, m + shift, level - 1), shift, lane)

    def tile(v, _):
        total = tree(v, 0, 5)
        for g in range(GROUP):
            out_ref[g, pl.ds(pl.multiple_of(v * 8, 8), 8), :] = total
        return 0

    lax.fori_loop(0, TX, tile, 0, unroll=2)

    squares = prints_ref[...] * prints_ref[...]
    energy = lax.dot_general(
        jnp.ones((8, 128), F32),
        squares,
        (((1,), (1,)), ((), ())),
        precision=lax.Precision.HIGHEST,
        preferred_element_type=F32,
    )
    rows = energy[:, 0:128]
    for q in range(1, 4):
        rows = jnp.where(sub == q, energy[:, 128 * q : 128 * q + 128], rows)
    for g in range(GROUP):
        out_ref[g, 64:72, :] = rows


def trace_kernel(
    parts_ref, old_ref, movie_ref, wide_ref, near_ref, places_ref, new_ref, weight_ref, field_ref, up_ref, down_ref
):
    sub, lane = iotas()
    start_field(movie_ref, field_ref)

    def total(start):
        rows = pl.ds(start, 8)
        value = parts_ref[0, rows, :]
        for g in range(1, GROUP):
            value = value + parts_ref[g, rows, :]
        return value

    energy = total(64)
    m = lane & 31
    own = (m >> 2) * 8 + (m & 3) + jnp.where(sub < 4, 0, 4)
    for v in range(TX):
        scale = pick_lanes(jnp.broadcast_to(energy[v // 2 : v // 2 + 1], (8, 128)), own + 64 * (v % 2))
        value = jnp.maximum(old_ref[v] + total(8 * v) / (scale + RIDGE), 0.0)
        new_ref[v] = value
        power = value * value
        power = power + pltpu.roll(power, 64, 1)
        power = power + pltpu.roll(power, 32, 1)
        power = merge_rows(power, power, 1, sub)
        power = merge_rows(power, power, 2, sub)
        weight_ref[v] = value / (power + RIDGE)
    subtract_all(new_ref, wide_ref, places_ref, field_ref)
    show_edges(field_ref, near_ref, up_ref, down_ref)


def improve_prints(
    above_ref, below_ref, weight_ref, prints_ref, near_ref, places_ref, whole_ref, new_ref, after=lambda v: None
):
    sub, lane = iotas()
    add_halo(whole_ref, above_ref, below_ref, near_ref)

    def tile(v, _):
        value = weight_ref[v]

        def eight(q, _):
            base = pl.multiple_of(v * OWNED + q * 8, 8)
            terms = []
            for b in range(4):
                pair = spread(value, q * 4 + b, sub, lane)
                for half in range(2):
                    for at in patch(v, q * 8 + half * 4 + b, places_ref):
                        terms.append(pair[half] * whole_ref[at, :])
            sides = []
            for n in range(4):
                low = merge_rows(terms[n], terms[4 + n], 1, sub)
                high = merge_rows(terms[8 + n], terms[12 + n], 1, sub)
                sides.append(merge_rows(low, high, 2, sub))
            step = merge_lanes(
                merge_lanes(sides[0], sides[1], 64, lane), merge_lanes(sides[2], sides[3], 64, lane), 32, lane
            )
            turned = pltpu.roll(step, 4, 0)
            dx = (lane & 32) != 0
            swapped = jnp.where(dx, pltpu.roll(turned, 32, 1), pltpu.roll(turned, 96, 1))
            step = jnp.where(dx == (sub >= 4), step, swapped)
            new_ref[pl.ds(base, 8), :] = jnp.maximum(prints_ref[pl.ds(base, 8), :] + step, 0.0)
            return 0

        lax.fori_loop(0, 8, eight, 0, unroll=8)
        after(v)
        return 0

    lax.fori_loop(0, TX, tile, 0)


def print_kernel(
    old_ref, above_ref, below_ref, weight_ref, activity_ref, movie_ref, prints_ref, near_ref, places_ref,
    new_ref, wide_ref, next_ref, up_ref, down_ref, whole_ref,
):
    improve_prints(above_ref, below_ref, weight_ref, prints_ref, near_ref, places_ref, whole_ref, new_ref)
    widen(new_ref[...], wide_ref)
    start_field(movie_ref, next_ref)
    subtract_all(activity_ref, wide_ref, places_ref, next_ref)
    show_edges(next_ref, near_ref, up_ref, down_ref)


def last_kernel(
    old_ref, above_ref, below_ref, weight_ref, prints_ref, near_ref, places_ref, out_ref, whole_ref, new_ref, sems
):
    def copy(v, z):
        rows = new_ref.at[pl.ds(pl.multiple_of(v * OWNED, OWNED), OWNED)]
        return pltpu.make_async_copy(rows, out_ref.at[v * TA + z], sems.at[v * TA + z])

    def send(v):
        for z in range(TA):
            copy(v, z).start()

    improve_prints(above_ref, below_ref, weight_ref, prints_ref, near_ref, places_ref, whole_ref, new_ref, send)
    for v in range(TX):
        for z in range(TA):
            copy(v, z).wait()


def swap_lanes(parts, lane):
    for shift in (1, 2):
        high = (lane & (32 * shift)) != 0
        turned = []
        for b in range(4):
            other = pltpu.roll(parts[b ^ shift], 32 * shift if b & shift == 0 else 128 - 32 * shift, 1)
            turned.append(jnp.where(high, other, parts[b]) if b & shift == 0 else jnp.where(high, parts[b], other))
        parts = turned
    return parts


def finish_kernel(blocks_ref, out_ref, rows_ref, sems):
    lane = lax.broadcasted_iota(jnp.int32, (OWNED, 128), 1)
    copies = []
    for z in range(TA):
        for a in range(2):
            rows = swap_lanes([blocks_ref[(4 * a + b) * TA + z] for b in range(4)], lane)
            for d in range(4):
                at = len(copies)
                rows_ref[at] = rows[d]
                columns = pl.ds(d * 1024 + (z * 2 + a) * 128, 128)
                copies.append(pltpu.make_async_copy(rows_ref.at[at], out_ref.at[:, columns], sems.at[at]))
                copies[-1].start()
    for copy in copies:
        copy.wait()


def shape(*sizes, dtype=F32):
    return jax.ShapeDtypeStruct(sizes, dtype)


def call(kernel, outs, places, scratch=(), smem=(), alias=None, left=()):
    return pl.pallas_call(
        kernel,
        out_shape=list(outs),
        in_specs=[SMEM if at in smem else VMEM for at in range(places)],
        out_specs=[ANY if at in left else VMEM for at in range(len(outs))],
        scratch_shapes=list(scratch),
        input_output_aliases={} if alias is None else {0: alias},
        compiler_params=pltpu.CompilerParams(vmem_limit_bytes=16 << 20),
    )


FIELD_SHAPE = shape(FIELD, 128)
EDGE_SHAPE = shape(2 * ROW, 128)
WIDE_SHAPE = shape(4, COUNT, 128)
AXES = ("tx", "ta")


def exchange(blocks):
    return lax.all_to_all(blocks, AXES, 0, 0, tiled=True)


def halo(near, far):
    near = lax.ppermute(near, "ty", [(0, 1), (1, 0), (2, 3), (3, 2)])
    return near, lax.ppermute(far, "ty", [(1, 2), (2, 1)])


def shards(movie, footprints, traces, anchor_row, anchor_col):
    layer = lax.axis_index("ta")
    column = lax.axis_index("tx")
    frames = traces.shape[0]
    index = lax.axis_index("ty")
    near = (index % 2).reshape(1)
    blocks = movie.reshape(frames, 4, CELL_ROWS, TX, 2, 128).transpose(3, 1, 2, 0, 4, 5)
    own = traces.reshape(frames, 8, 2, 4).transpose(2, 0, 1, 3).reshape(2, 128)
    spots = jnp.concatenate([anchor_row, anchor_col]).astype(F32).reshape(1, 128)
    got = exchange(
        call(
            pack_kernel,
            (shape(GROUP, 168, 128, dtype=jnp.bfloat16),),
            4,
            smem=(3,),
        )(
            blocks.reshape(GROUP, 128, 128), footprints, jnp.concatenate([own, spots]), layer.reshape(1)
        )[0]
    )
    cells, prints, activity, places = call(
        unpack_kernel,
        (shape(INNER, 128), shape(COUNT, 128), shape(TX, 8, 128), shape(TX, 128, dtype=jnp.int32)),
        1,
    )(got)
    wide, field, up, down = call(
        first_kernel, (WIDE_SHAPE, FIELD_SHAPE, EDGE_SHAPE, EDGE_SHAPE), 5, smem=(3, 4)
    )(cells, prints, activity, near, places)
    for sweep in range(ITERS):
        above, below = halo(up, down)
        sums, _ = call(update_kernel, (shape(GROUP, 72, 128), FIELD_SHAPE), 7, smem=(5, 6), alias=1)(
            field, above, below, prints, wide, near, places
        )
        parts = exchange(sums)
        activity, weight, field, up, down = call(
            trace_kernel,
            (shape(TX, 8, 128), shape(TX, 8, 128), FIELD_SHAPE, EDGE_SHAPE, EDGE_SHAPE),
            6,
            smem=(4, 5),
        )(parts, activity, cells, wide, near, places)
        above, below = halo(up, down)
        if sweep + 1 < ITERS:
            prints, wide, field, up, down, _ = call(
                print_kernel,
                (shape(COUNT, 128), WIDE_SHAPE, FIELD_SHAPE, EDGE_SHAPE, EDGE_SHAPE, FIELD_SHAPE),
                9,
                smem=(7, 8),
                alias=5,
            )(field, above, below, weight, activity, cells, prints, near, places)
        else:
            sent, _ = call(
                last_kernel,
                (shape(GROUP, OWNED, 128), FIELD_SHAPE),
                7,
                (pltpu.VMEM((COUNT, 128), F32), pltpu.SemaphoreType.DMA((GROUP,))),
                left=(0,),
                smem=(5, 6),
                alias=1,
            )(field, above, below, weight, prints, near, places)
    footprints_out = call(
        finish_kernel,
        (shape(OWNED, 4096),),
        1,
        (pltpu.VMEM((GROUP, OWNED, 128), F32), pltpu.SemaphoreType.DMA((GROUP,))),
        left=(0,),
    )(exchange(sent))[0]
    mine = lax.dynamic_index_in_dim(activity, column, 0, keepdims=False).reshape(2, TA, 128)
    mine = lax.dynamic_index_in_dim(mine, layer, 1, keepdims=False)
    traces_out = mine.reshape(2, frames, 8, 4).transpose(1, 2, 0, 3).reshape(frames, OWNED)
    return footprints_out, traces_out


def solution(mesh):
    placed = (
        P("ta", None, "ty", "tx"),
        P(("ty", "tx"), None),
        P("ta", ("ty", "tx")),
        P(("ty", "tx")),
        P(("ty", "tx")),
    )
    return jax.shard_map(
        shards,
        mesh=mesh,
        in_specs=placed,
        out_specs=(P(("ty", "tx"), None), P("ta", ("ty", "tx"))),
        check_vma=False,
    )
```

```python
import functools

import jax
import jax.numpy as jnp
from jax import lax
from jax.experimental import pallas as pl
from jax.experimental.pallas import tpu as pltpu
from jax.sharding import PartitionSpec as P

ITERS = 2
RIDGE = 1.0
TX = 8
TA = 4
GROUP = TX * TA
OWNED = 64
COUNT = TX * OWNED
ROW = (TX * 8 + 2) * TA
CELL_ROWS = 16
FIELD = (CELL_ROWS + 2) * ROW
INNER = CELL_ROWS * ROW
VMEM = pl.BlockSpec(memory_space=pltpu.VMEM)
SMEM = pl.BlockSpec(memory_space=pltpu.SMEM)
ANY = pl.BlockSpec(memory_space=pl.ANY)
F32 = jnp.float32


def iotas():
    return (
        lax.broadcasted_iota(jnp.int32, (8, 128), 0),
        lax.broadcasted_iota(jnp.int32, (8, 128), 1),
    )


def pick_lanes(value, index):
    return jnp.take_along_axis(value, index, axis=1, mode="promise_in_bounds")


def pick_rows(value, index):
    return jnp.take_along_axis(value, index, axis=0, mode="promise_in_bounds")


def merge_lanes(first, second, shift, lane):
    if shift == 64:
        high = lane >= 64
        return jnp.where(high, second, first) + pltpu.roll(jnp.where(high, first, second), 64, 1)
    return jnp.where(
        (lane & shift) != 0,
        second + pltpu.roll(second, shift, 1),
        first + pltpu.roll(first, 128 - shift, 1),
    )


def merge_rows(first, second, shift, sub):
    return jnp.where(
        (sub & shift) != 0,
        second + pltpu.roll(second, shift, 0),
        first + pltpu.roll(first, 8 - shift, 0),
    )


def spread(value, m, sub, lane):
    wide = pick_lanes(value, (lane & 96) + m)
    turned = pltpu.roll(wide, 4, 0)
    low = sub < 4
    return jnp.where(low, wide, turned), jnp.where(low, turned, wide)


def pieces(value, count):
    out = []
    for _ in range(count):
        out.append(value.astype(jnp.bfloat16))
        value = value - out[-1].astype(F32)
    return out


def widen(prints, wide_ref):
    source = lax.broadcasted_iota(jnp.int32, (384, 512), 0) & 127
    target = lax.broadcasted_iota(jnp.int32, (384, 512), 1)
    copies = (source == (target >> 7) * 32 + (target & 31)).astype(jnp.bfloat16)
    parts = jnp.concatenate(pieces(prints, 3), axis=1)
    wide = jnp.dot(parts, copies, preferred_element_type=F32)
    for d in range(4):
        wide_ref[d] = wide[:, 128 * d : 128 * d + 128]


def print_pair(wide_ref, neuron, sub):
    rows = [jnp.broadcast_to(wide_ref[d, pl.ds(neuron, 1), :], (8, 128)) for d in range(4)]
    return jnp.where(sub < 4, rows[0], rows[1]), jnp.where(sub < 4, rows[2], rows[3])


def patch(v, k, places_ref):
    start = pl.multiple_of(places_ref[v, k], 4)
    return pl.ds(start, 8), pl.ds(start + ROW, 8)


def subtract_some(activity_ref, wide_ref, table_ref, field_ref, count, group_of):
    sub, lane = iotas()
    for first in range(2):
        tiles = [first + 2 * t for t in range(4)]
        values = [activity_ref[v] for v in tiles]

        def some(at, _):
            q = group_of(at)
            for b in range(4):
                pairs = [spread(value, q * 4 + b, sub, lane) for value in values]
                for half in range(2):
                    spots, changed = [], []
                    for v, pair in zip(tiles, pairs):
                        k = q * 8 + half * 4 + b
                        for at, side in zip(patch(v, k, table_ref), print_pair(wide_ref, v * OWNED + k, sub)):
                            spots.append(at)
                            changed.append(field_ref[at, :] - pair[half] * side)
                    for at, value in zip(spots, changed):
                        field_ref[at, :] = value
            return 0

        lax.fori_loop(0, count, some, 0)


def subtract_outer(activity_ref, wide_ref, table_ref, field_ref):
    start, stop = table_ref[16, 4], table_ref[16, 5]
    subtract_some(
        activity_ref,
        wide_ref,
        table_ref,
        field_ref,
        start + 8 - stop,
        lambda at: at + jnp.where(at >= start, stop - start, 0),
    )


def subtract_inner(activity_ref, wide_ref, table_ref, field_ref):
    start, stop = table_ref[16, 4], table_ref[16, 5]
    subtract_some(activity_ref, wide_ref, table_ref, field_ref, stop - start, lambda at: at + start)


def start_field(movie_ref, field_ref):
    field_ref[0:ROW, :] = jnp.zeros((ROW, 128), F32)
    field_ref[ROW + INNER :, :] = jnp.zeros((ROW, 128), F32)

    def one(r, _):
        field_ref[pl.ds((r + 1) * ROW, ROW), :] = movie_ref[pl.ds(r * ROW, ROW), :]
        return 0

    lax.fori_loop(0, CELL_ROWS, one, 0)


def add_edge(field_ref, edge_ref, low):
    rows = pl.ds(pl.multiple_of(jnp.where(low, INNER, 0), 8), 2 * ROW)
    field_ref[rows, :] += edge_ref[...]


def show_edges(field_ref, near_ref, near_out, far_out):
    even = near_ref[0] == 0
    top = field_ref[0 : 2 * ROW, :]
    bottom = field_ref[INNER:, :]
    near_out[...] = jnp.where(even, bottom, top)
    far_out[...] = jnp.where(even, top, bottom)


def pack_kernel(cells_ref, prints_ref, small_ref, layer_ref, out_ref, ranks_ref):
    lane = lax.broadcasted_iota(jnp.int32, (16, 128), 1)
    rows = pl.ds(pl.multiple_of(layer_ref[0] * 16, 16), 16)
    down = lax.broadcasted_iota(jnp.int32, (OWNED, OWNED), 0)
    right = lax.broadcasted_iota(jnp.int32, (OWNED, OWNED), 1)
    theirs = jnp.broadcast_to(small_ref[4:5, :], (OWNED, OWNED))
    ours = dot((down == right).astype(F32), theirs, 1)
    before = (theirs < ours) | ((theirs == ours) & (right < down))
    ranks = jnp.sum(before.astype(F32), axis=1, keepdims=True).astype(jnp.int32)
    order = (right == ranks).astype(F32)
    names = right[0:1].astype(F32)
    tail = [piece.astype(F32) for piece in pieces(small_ref[0:4, :], 3)]
    tail = dot(jnp.concatenate(tail + [small_ref[4:6, :], names, jnp.zeros((1, OWNED), F32)], axis=0), order, 0)
    tail = jnp.concatenate([tail[0:8], tail[8:16]], axis=1)
    tail = jnp.concatenate([tail, tail], axis=0).astype(jnp.bfloat16)
    places = dot(jnp.broadcast_to(names, (8, OWNED)), order, 1)
    ranks_ref[...] = jnp.concatenate([places, jnp.zeros((8, OWNED), F32)], axis=1).astype(jnp.int32)
    for a in range(8):
        blocks = swap_lanes(
            [prints_ref[rows, d * 1024 + a * 128 : d * 1024 + a * 128 + 128] for d in range(4)], lane
        )
        for b in range(4):
            shard = 4 * a + b
            dest = (shard % TX) * TA + shard // TX
            out_ref[dest, 0:128, :] = cells_ref[dest]
            for at, piece in enumerate(pieces(blocks[b], 2)):
                out_ref[dest, 128 + 16 * at : 144 + 16 * at, :] = piece
            out_ref[dest, 160:168, :] = tail[0:8]


def dot(left, right, axis):
    return lax.dot_general(left, right, (((1,), (axis,)), ((), ())), preferred_element_type=F32)


def own_lanes(sub, lane):
    m = lane & 31
    return (m >> 2) * 8 + (m & 3) + jnp.where(sub < 4, 0, 4)


def unpack_kernel(got_ref, near_ref, movie_ref, prints_ref, activity_ref, table_ref):
    sub, lane = iotas()
    skew = (lane - 16 * sub) & 127
    turn = ((lane >> 4) - sub) & 7
    back = (lane + 16 * sub) & 127
    for r in range(CELL_ROWS):
        movie_ref[r * ROW : r * ROW + 8, :] = jnp.zeros((8, 128), F32)
        movie_ref[(r + 1) * ROW - 8 : (r + 1) * ROW, :] = jnp.zeros((8, 128), F32)

    def block(g, _):
        base = (1 + 8 * (g // TA)) * TA + g % TA
        for t in range(8):
            both = got_ref[g, 16 * t : 16 * t + 16, :].astype(F32)
            for h in range(2):
                value = both[8 * h : 8 * h + 8]
                value = pick_lanes(pick_rows(pick_lanes(value, skew), turn), back)
                movie_ref[pl.ds(base + (2 * t + h) * ROW, 8, stride=TA), :] = value
        high, low = [got_ref[g, 128 + 16 * at : 144 + 16 * at, :].astype(F32) for at in range(2)]
        prints_ref[pl.ds(pl.multiple_of(g * 16, 16), 16), :] = high + low
        return 0

    lax.fori_loop(0, GROUP, block, 0, unroll=2)
    own = own_lanes(sub, lane)
    found = []
    for v in range(TX):
        tails = [got_ref[v * TA + z, 160:168, :].astype(F32) for z in range(TA)]
        turned = [pltpu.roll(tail, 64, 1) for tail in tails]
        values = [tail[0:4] + (tail[4:8] + other[0:4]) for tail, other in zip(tails, turned)]
        activity = jnp.zeros((8, 128), F32)
        for f in range(4):
            rows = jnp.concatenate([value[f : f + 1] for value in values] * 2, axis=0)
            activity = jnp.where((lane >> 5) == f, pick_lanes(rows, own), activity)
        activity_ref[v] = activity
        found.append(turned[0][4:7])
    row, col, name = [jnp.concatenate([one[at : at + 1] for one in found], axis=0) for at in range(3)]
    table_ref[0:8, :] = ((row + 1) * ROW + (col + (8 * sub.astype(F32) + 1)) * TA).astype(jnp.int32)
    table_ref[8:16, :] = name.astype(jnp.int32)
    real = lane < OWNED

    def most(mask):
        count = jnp.sum(jnp.where(real & mask, 1.0, 0.0), axis=1, keepdims=True)
        return jnp.max(count, axis=0, keepdims=True).astype(jnp.int32)

    top = (most(row < 0.5) + 7) >> 3
    bottom = (OWNED - most(row > 13.5)) >> 3
    even = near_ref[0] == 0
    limits = (
        jnp.where(even, top, 0),
        jnp.where(even, 8, bottom),
        jnp.where(even, 0, bottom),
        jnp.where(even, top, 8),
        top,
        jnp.maximum(top, bottom),
    )
    line = jnp.zeros((8, 128), jnp.int32)
    for at, limit in enumerate(limits):
        line = jnp.where(lane == at, limit, line)
    table_ref[16:24, :] = line


def first_kernel(
    movie_ref, raw_ref, activity_ref, near_ref, table_ref, prints_ref, wide_ref, field_ref, up_ref, down_ref
):
    def some(q, _):
        for v in range(TX):
            rows = [raw_ref[pl.ds(v * OWNED + table_ref[8 + v, q * 8 + n], 1), :] for n in range(8)]
            prints_ref[pl.ds(pl.multiple_of(v * OWNED + q * 8, 8), 8), :] = jnp.concatenate(rows, axis=0)
        return 0

    lax.fori_loop(0, 8, some, 0)
    widen(prints_ref[...], wide_ref)
    start_field(movie_ref, field_ref)
    subtract_outer(activity_ref, wide_ref, table_ref, field_ref)
    show_edges(field_ref, near_ref, up_ref, down_ref)


def fold_updates(field_ref, wide_ref, table_ref, part_ref, first, last):
    sub, lane = iotas()

    def leaf(v, q, b):
        folded = []
        for half in range(2):
            k = q * 8 + half * 4 + b
            upper, lower = print_pair(wide_ref, v * OWNED + k, sub)
            top, bottom = patch(v, k, table_ref)
            value = upper * field_ref[top, :] + lower * field_ref[bottom, :]
            folded.append(value + pltpu.roll(value, 4, 0))
        return jnp.where(sub < 4, folded[0], folded[1])

    def eight(q, _):
        for v in range(TX):
            low = merge_lanes(leaf(v, q, 0), leaf(v, q, 1), 1, lane)
            high = merge_lanes(leaf(v, q, 2), leaf(v, q, 3), 1, lane)
            part_ref[v * 8 + q] = merge_lanes(low, high, 2, lane)
        return 0

    lax.fori_loop(first, last, eight, 0)


def early_update_kernel(
    old_ref, near_ref_in, activity_ref, wide_ref, near_ref, table_ref, field_ref, part_ref
):
    subtract_inner(activity_ref, wide_ref, table_ref, field_ref)
    add_edge(field_ref, near_ref_in, near_ref[0] == 0)
    fold_updates(field_ref, wide_ref, table_ref, part_ref, table_ref[16, 0], table_ref[16, 1])


def update_kernel(
    old_ref, early_ref, far_ref, prints_ref, wide_ref, near_ref, table_ref, out_ref, field_ref, part_ref
):
    sub, lane = iotas()
    add_edge(field_ref, far_ref, near_ref[0] != 0)
    fold_updates(field_ref, wide_ref, table_ref, part_ref, table_ref[16, 2], table_ref[16, 3])
    for v in range(TX):
        parts = [part_ref[v * 8 + q] for q in range(8)]
        for shift in (4, 8, 16):
            parts = [merge_lanes(parts[n], parts[n + 1], shift, lane) for n in range(0, len(parts), 2)]
        for g in range(GROUP):
            out_ref[g, 8 * v : 8 * v + 8, :] = parts[0]
    squares = prints_ref[...] * prints_ref[...]
    energy = lax.dot_general(
        jnp.ones((8, 128), F32),
        squares,
        (((1,), (1,)), ((), ())),
        precision=lax.Precision.HIGHEST,
        preferred_element_type=F32,
    )
    rows = energy[:, 0:128]
    for q in range(1, 4):
        rows = jnp.where(sub == q, energy[:, 128 * q : 128 * q + 128], rows)
    for g in range(GROUP):
        out_ref[g, 64:72, :] = rows


def trace_kernel(
    parts_ref, old_ref, movie_ref, wide_ref, near_ref, places_ref, new_ref, weight_ref, field_ref, up_ref, down_ref
):
    sub, lane = iotas()
    start_field(movie_ref, field_ref)

    def total(start):
        rows = pl.ds(start, 8)
        value = parts_ref[0, rows, :]
        for g in range(1, GROUP):
            value = value + parts_ref[g, rows, :]
        return value

    energy = total(64)
    own = own_lanes(sub, lane)
    for v in range(TX):
        scale = pick_lanes(jnp.broadcast_to(energy[v // 2 : v // 2 + 1], (8, 128)), own + 64 * (v % 2))
        value = jnp.maximum(old_ref[v] + total(8 * v) / (scale + RIDGE), 0.0)
        new_ref[v] = value
        power = value * value
        power = power + pltpu.roll(power, 64, 1)
        power = power + pltpu.roll(power, 32, 1)
        power = merge_rows(power, power, 1, sub)
        power = merge_rows(power, power, 2, sub)
        weight_ref[v] = value / (power + RIDGE)
    subtract_outer(new_ref, wide_ref, places_ref, field_ref)
    show_edges(field_ref, near_ref, up_ref, down_ref)


def improve_prints(weight_ref, prints_ref, table_ref, field_ref, new_ref, first, last):
    sub, lane = iotas()

    def one(v, q):
        base = pl.multiple_of(v * OWNED + q * 8, 8)
        terms = []
        for b in range(4):
            pair = spread(weight_ref[v], q * 4 + b, sub, lane)
            for half in range(2):
                for at in patch(v, q * 8 + half * 4 + b, table_ref):
                    terms.append(pair[half] * field_ref[at, :])
        sides = []
        for n in range(4):
            low = merge_rows(terms[n], terms[4 + n], 1, sub)
            high = merge_rows(terms[8 + n], terms[12 + n], 1, sub)
            sides.append(merge_rows(low, high, 2, sub))
        step = merge_lanes(
            merge_lanes(sides[0], sides[1], 64, lane), merge_lanes(sides[2], sides[3], 64, lane), 32, lane
        )
        turned = pltpu.roll(step, 4, 0)
        dx = (lane & 32) != 0
        swapped = jnp.where(dx, pltpu.roll(turned, 32, 1), pltpu.roll(turned, 96, 1))
        step = jnp.where(dx == (sub >= 4), step, swapped)
        new_ref[pl.ds(base, 8), :] = jnp.maximum(prints_ref[pl.ds(base, 8), :] + step, 0.0)

    def eight(q, _):
        for v in range(TX):
            one(v, q)
        return 0

    lax.fori_loop(first, last, eight, 0)


def early_print_kernel(
    old_ref, near_ref_in, activity_ref, wide_ref, weight_ref, prints_ref, near_ref, table_ref, field_ref, new_ref
):
    subtract_inner(activity_ref, wide_ref, table_ref, field_ref)
    add_edge(field_ref, near_ref_in, near_ref[0] == 0)
    improve_prints(weight_ref, prints_ref, table_ref, field_ref, new_ref, table_ref[16, 0], table_ref[16, 1])


def finish_prints(far_ref, weight_ref, prints_ref, near_ref, table_ref, field_ref, new_ref):
    add_edge(field_ref, far_ref, near_ref[0] != 0)
    improve_prints(weight_ref, prints_ref, table_ref, field_ref, new_ref, table_ref[16, 2], table_ref[16, 3])


def print_kernel(
    old_ref, early_ref, far_ref, weight_ref, activity_ref, movie_ref, prints_ref, near_ref, table_ref,
    field_ref, new_ref, wide_ref, next_ref, up_ref, down_ref,
):
    finish_prints(far_ref, weight_ref, prints_ref, near_ref, table_ref, field_ref, new_ref)
    widen(new_ref[...], wide_ref)
    start_field(movie_ref, next_ref)
    subtract_outer(activity_ref, wide_ref, table_ref, next_ref)
    show_edges(next_ref, near_ref, up_ref, down_ref)


def last_kernel(
    old_ref, early_ref, far_ref, weight_ref, prints_ref, near_ref, table_ref,
    field_ref, new_ref, out_ref, raw_ref, sems,
):
    finish_prints(far_ref, weight_ref, prints_ref, near_ref, table_ref, field_ref, new_ref)
    copies = []

    def some(q, _):
        for v in range(TX):
            rows = new_ref[pl.ds(pl.multiple_of(v * OWNED + q * 8, 8), 8), :]
            for n in range(8):
                raw_ref[pl.ds(v * OWNED + table_ref[8 + v, q * 8 + n], 1), :] = rows[n : n + 1]
        return 0

    lax.fori_loop(0, 8, some, 0)
    for v in range(TX):
        for z in range(TA):
            rows = raw_ref.at[pl.ds(v * OWNED, OWNED)]
            copies.append(pltpu.make_async_copy(rows, out_ref.at[v * TA + z], sems.at[v * TA + z]))
            copies[-1].start()
    for copy in copies:
        copy.wait()


def traces_kernel(activity_ref, ranks_ref, spot_ref, out_ref):
    sub, lane = iotas()
    value = activity_ref[spot_ref[0]]
    ranks = ranks_ref[...]
    m = (ranks >> 3) * 4 + (ranks & 3)
    mine = sub == ((ranks >> 2) & 1) * 4 + spot_ref[1]
    for f in range(4):
        found = jnp.where(mine, pick_lanes(value, f * 32 + m), 0.0)
        out_ref[f : f + 1, :] = jnp.sum(found, axis=0, keepdims=True)[:, 0:OWNED]


def swap_lanes(parts, lane):
    for shift in (1, 2):
        high = (lane & (32 * shift)) != 0
        turned = []
        for b in range(4):
            other = pltpu.roll(parts[b ^ shift], 32 * shift if b & shift == 0 else 128 - 32 * shift, 1)
            turned.append(jnp.where(high, other, parts[b]) if b & shift == 0 else jnp.where(high, parts[b], other))
        parts = turned
    return parts


def finish_kernel(blocks_ref, out_ref, rows_ref, sems):
    lane = lax.broadcasted_iota(jnp.int32, (OWNED, 128), 1)
    copies = []
    for z in range(TA):
        for a in range(2):
            rows = swap_lanes([blocks_ref[(4 * a + b) * TA + z] for b in range(4)], lane)
            for d in range(4):
                at = len(copies)
                rows_ref[at] = rows[d]
                columns = pl.ds(d * 1024 + (z * 2 + a) * 128, 128)
                copies.append(pltpu.make_async_copy(rows_ref.at[at], out_ref.at[:, columns], sems.at[at]))
                copies[-1].start()
    for copy in copies:
        copy.wait()


def shape(*sizes, dtype=F32):
    return jax.ShapeDtypeStruct(sizes, dtype)


def call(kernel, outs, operands, scratch=(), smem=(), alias=(), left=(), work=1):
    return pl.pallas_call(
        kernel,
        out_shape=list(outs),
        in_specs=[SMEM if at in smem else VMEM for at in range(operands)],
        out_specs=[ANY if at in left else VMEM for at in range(len(outs))],
        scratch_shapes=list(scratch),
        input_output_aliases=dict(alias),
        compiler_params=pltpu.CompilerParams(vmem_limit_bytes=16 << 20),
        cost_estimate=pl.CostEstimate(flops=work << 20, bytes_accessed=work << 20, transcendentals=0),
    )


FIELD_SHAPE = shape(FIELD, 128)
EDGE_SHAPE = shape(2 * ROW, 128)
PRINT_SHAPE = shape(COUNT, 128)
TRACE_SHAPE = shape(TX, 8, 128)
WIDE_SHAPE = shape(4, COUNT, 128)
AXES = ("tx", "ta")


def exchange(blocks):
    return lax.all_to_all(blocks, AXES, 0, 0, tiled=True)


def halo(near, far):
    near = lax.ppermute(near, "ty", [(0, 1), (1, 0), (2, 3), (3, 2)])
    return near, lax.ppermute(far, "ty", [(1, 2), (2, 1)])


def shards(movie, footprints, traces, anchor_row, anchor_col):
    layer = lax.axis_index("ta")
    column = lax.axis_index("tx")
    frames = traces.shape[0]
    near = (lax.axis_index("ty") % 2).reshape(1)
    blocks = movie.reshape(frames, 4, CELL_ROWS, TX, 2, 128).transpose(3, 1, 2, 0, 4, 5)
    small = jnp.concatenate([traces, jnp.stack([anchor_row, anchor_col]).astype(F32)])
    sent, ranks = call(
        pack_kernel, (shape(GROUP, 168, 128, dtype=jnp.bfloat16), shape(8, 128, dtype=jnp.int32)), 4, smem=(3,)
    )(blocks.reshape(GROUP, 128, 128), footprints, small, layer.reshape(1))
    cells, raw, activity, table = call(
        unpack_kernel,
        (shape(INNER, 128), PRINT_SHAPE, TRACE_SHAPE, shape(24, 128, dtype=jnp.int32)),
        2,
        smem=(1,),
    )(exchange(sent), near)
    prints, wide, field, left, right = call(
        first_kernel, (PRINT_SHAPE, WIDE_SHAPE, FIELD_SHAPE, EDGE_SHAPE, EDGE_SHAPE), 5, smem=(3, 4)
    )(cells, raw, activity, near, table)
    for sweep in range(ITERS):
        left, right = halo(left, right)
        field, part = call(
            early_update_kernel, (FIELD_SHAPE, shape(64, 8, 128)), 6, smem=(4, 5), alias=((0, 0),), work=8
        )(field, left, activity, wide, near, table)
        sums, _, _ = call(
            update_kernel,
            (shape(GROUP, 72, 128), FIELD_SHAPE, shape(64, 8, 128)),
            7,
            smem=(5, 6),
            alias=((0, 1), (1, 2)),
        )(field, part, right, prints, wide, near, table)
        activity, weight, field, left, right = call(
            trace_kernel, (TRACE_SHAPE, TRACE_SHAPE, FIELD_SHAPE, EDGE_SHAPE, EDGE_SHAPE), 6, smem=(4, 5)
        )(exchange(sums), activity, cells, wide, near, table)
        left, right = halo(left, right)
        field, new = call(early_print_kernel, (FIELD_SHAPE, PRINT_SHAPE), 8, smem=(6, 7), alias=((0, 0),), work=8)(
            field, left, activity, wide, weight, prints, near, table
        )
        if sweep + 1 < ITERS:
            _, prints, wide, field, left, right = call(
                print_kernel,
                (FIELD_SHAPE, PRINT_SHAPE, WIDE_SHAPE, FIELD_SHAPE, EDGE_SHAPE, EDGE_SHAPE),
                9,
                smem=(7, 8),
                alias=((0, 0), (1, 1)),
            )(field, new, right, weight, activity, cells, prints, near, table)
        else:
            _, _, sent = call(
                last_kernel,
                (FIELD_SHAPE, PRINT_SHAPE, shape(GROUP, OWNED, 128)),
                7,
                (pltpu.VMEM((COUNT, 128), F32), pltpu.SemaphoreType.DMA((GROUP,))),
                smem=(5, 6),
                alias=((0, 0), (1, 1)),
                left=(2,),
            )(field, new, right, weight, prints, near, table)
    footprints_out = call(
        finish_kernel,
        (shape(OWNED, 4096),),
        1,
        (pltpu.VMEM((GROUP, OWNED, 128), F32), pltpu.SemaphoreType.DMA((GROUP,))),
        left=(0,),
    )(exchange(sent))[0]
    traces_out = call(traces_kernel, (shape(4, OWNED),), 3, smem=(2,))(activity, ranks, jnp.stack([column, layer]))[0]
    return footprints_out, traces_out


def solution(mesh):
    placed = (
        P("ta", None, "ty", "tx"),
        P(("ty", "tx"), None),
        P("ta", ("ty", "tx")),
        P(("ty", "tx")),
        P(("ty", "tx")),
    )
    return jax.shard_map(
        shards,
        mesh=mesh,
        in_specs=placed,
        out_specs=(P(("ty", "tx"), None), P("ta", ("ty", "tx"))),
        check_vma=False,
    )
```

```python
import functools

import jax
import jax.numpy as jnp
from jax import lax
from jax.experimental import pallas as pl
from jax.experimental.pallas import tpu as pltpu
from jax.sharding import PartitionSpec as P

ITERS = 2
RIDGE = 1.0
TX = 8
TA = 4
GROUP = TX * TA
OWNED = 64
COUNT = TX * OWNED
ROW = (TX * 8 + 2) * TA
CELL_ROWS = 16
FIELD = (CELL_ROWS + 2) * ROW
INNER = CELL_ROWS * ROW
VMEM = pl.BlockSpec(memory_space=pltpu.VMEM)
SMEM = pl.BlockSpec(memory_space=pltpu.SMEM)
ANY = pl.BlockSpec(memory_space=pl.ANY)
F32 = jnp.float32


def iotas():
    return (
        lax.broadcasted_iota(jnp.int32, (8, 128), 0),
        lax.broadcasted_iota(jnp.int32, (8, 128), 1),
    )


def pick_lanes(value, index):
    return jnp.take_along_axis(value, index, axis=1, mode="promise_in_bounds")


def pick_rows(value, index):
    return jnp.take_along_axis(value, index, axis=0, mode="promise_in_bounds")


def merge_lanes(first, second, shift, lane):
    if shift == 64:
        high = lane >= 64
        return jnp.where(high, second, first) + pltpu.roll(jnp.where(high, first, second), 64, 1)
    return jnp.where(
        (lane & shift) != 0,
        second + pltpu.roll(second, shift, 1),
        first + pltpu.roll(first, 128 - shift, 1),
    )


def merge_rows(first, second, shift, sub):
    return jnp.where(
        (sub & shift) != 0,
        second + pltpu.roll(second, shift, 0),
        first + pltpu.roll(first, 8 - shift, 0),
    )


def spread(value, m, sub, lane):
    wide = pick_lanes(value, (lane & 96) + m)
    turned = pltpu.roll(wide, 4, 0)
    low = sub < 4
    return jnp.where(low, wide, turned), jnp.where(low, turned, wide)


def pieces(value, count):
    out = []
    for _ in range(count):
        out.append(value.astype(jnp.bfloat16))
        value = value - out[-1].astype(F32)
    return out


def widen(prints, wide_ref):
    source = lax.broadcasted_iota(jnp.int32, (384, 512), 0) & 127
    target = lax.broadcasted_iota(jnp.int32, (384, 512), 1)
    copies = (source == (target >> 7) * 32 + (target & 31)).astype(jnp.bfloat16)
    parts = jnp.concatenate(pieces(prints, 3), axis=1)
    wide = jnp.dot(parts, copies, preferred_element_type=F32)
    for d in range(4):
        wide_ref[d] = wide[:, 128 * d : 128 * d + 128]


def print_pair(wide_ref, neuron, sub):
    rows = [jnp.broadcast_to(wide_ref[d, pl.ds(neuron, 1), :], (8, 128)) for d in range(4)]
    return jnp.where(sub < 4, rows[0], rows[1]), jnp.where(sub < 4, rows[2], rows[3])


def patch(v, k, places_ref):
    start = pl.multiple_of(places_ref[v, k], 4)
    return pl.ds(start, 8), pl.ds(start + ROW, 8)


def subtract_some(activity_ref, wide_ref, table_ref, field_ref, count, group_of):
    sub, lane = iotas()
    for first in range(2):
        tiles = [first + 2 * t for t in range(4)]
        values = [activity_ref[v] for v in tiles]

        def some(at, _):
            q = group_of(at)
            for b in range(4):
                pairs = [spread(value, q * 4 + b, sub, lane) for value in values]
                for half in range(2):
                    spots, changed = [], []
                    for v, pair in zip(tiles, pairs):
                        k = q * 8 + half * 4 + b
                        for at, side in zip(patch(v, k, table_ref), print_pair(wide_ref, v * OWNED + k, sub)):
                            spots.append(at)
                            changed.append(field_ref[at, :] - pair[half] * side)
                    for at, value in zip(spots, changed):
                        field_ref[at, :] = value
            return 0

        lax.fori_loop(0, count, some, 0)


def subtract_outer(activity_ref, wide_ref, table_ref, field_ref):
    start, stop = table_ref[16, 4], table_ref[16, 5]
    subtract_some(
        activity_ref,
        wide_ref,
        table_ref,
        field_ref,
        start + 8 - stop,
        lambda at: at + jnp.where(at >= start, stop - start, 0),
    )


def subtract_inner(activity_ref, wide_ref, table_ref, field_ref):
    start, stop = table_ref[16, 4], table_ref[16, 5]
    subtract_some(activity_ref, wide_ref, table_ref, field_ref, stop - start, lambda at: at + start)


def start_field(movie_ref, field_ref):
    field_ref[0:ROW, :] = jnp.zeros((ROW, 128), F32)
    field_ref[ROW + INNER :, :] = jnp.zeros((ROW, 128), F32)

    def one(r, _):
        field_ref[pl.ds((r + 1) * ROW, ROW), :] = movie_ref[pl.ds(r * ROW, ROW), :]
        return 0

    lax.fori_loop(0, CELL_ROWS, one, 0)


def add_edge(field_ref, edge_ref, low):
    rows = pl.ds(pl.multiple_of(jnp.where(low, INNER, 0), 8), 2 * ROW)
    field_ref[rows, :] += edge_ref[...]


def show_edges(field_ref, near_ref, near_out, far_out):
    even = near_ref[0] == 0
    top = field_ref[0 : 2 * ROW, :]
    bottom = field_ref[INNER:, :]
    near_out[...] = jnp.where(even, bottom, top)
    far_out[...] = jnp.where(even, top, bottom)


def pack_kernel(cells_ref, prints_ref, small_ref, layer_ref, out_ref, ranks_ref):
    lane = lax.broadcasted_iota(jnp.int32, (16, 128), 1)
    rows = pl.ds(pl.multiple_of(layer_ref[0] * 16, 16), 16)
    down = lax.broadcasted_iota(jnp.int32, (OWNED, OWNED), 0)
    right = lax.broadcasted_iota(jnp.int32, (OWNED, OWNED), 1)
    theirs = jnp.broadcast_to(small_ref[4:5, :], (OWNED, OWNED))
    ours = dot((down == right).astype(F32), theirs, 1)
    before = (theirs < ours) | ((theirs == ours) & (right < down))
    ranks = jnp.sum(before.astype(F32), axis=1, keepdims=True).astype(jnp.int32)
    order = (right == ranks).astype(F32)
    names = right[0:1].astype(F32)
    tail = [piece.astype(F32) for piece in pieces(small_ref[0:4, :], 3)]
    tail = dot(jnp.concatenate(tail + [small_ref[4:6, :], names, jnp.zeros((1, OWNED), F32)], axis=0), order, 0)
    tail = jnp.concatenate([tail[0:8], tail[8:16]], axis=1)
    tail = jnp.concatenate([tail, tail], axis=0).astype(jnp.bfloat16)
    places = dot(jnp.broadcast_to(names, (8, OWNED)), order, 1)
    ranks_ref[...] = jnp.concatenate([places, jnp.zeros((8, OWNED), F32)], axis=1).astype(jnp.int32)
    for a in range(8):
        blocks = swap_lanes(
            [prints_ref[rows, d * 1024 + a * 128 : d * 1024 + a * 128 + 128] for d in range(4)], lane
        )
        for b in range(4):
            shard = 4 * a + b
            dest = (shard % TX) * TA + shard // TX
            out_ref[dest, 0:128, :] = cells_ref[dest]
            for at, piece in enumerate(pieces(blocks[b], 2)):
                out_ref[dest, 128 + 16 * at : 144 + 16 * at, :] = piece
            out_ref[dest, 160:168, :] = tail[0:8]


def dot(left, right, axis):
    return lax.dot_general(left, right, (((1,), (axis,)), ((), ())), preferred_element_type=F32)


def own_lanes(sub, lane):
    m = lane & 31
    return (m >> 2) * 8 + (m & 3) + jnp.where(sub < 4, 0, 4)


def unpack_kernel(got_ref, near_ref, movie_ref, prints_ref, activity_ref, table_ref):
    sub, lane = iotas()
    skew = (lane - 16 * sub) & 127
    turn = ((lane >> 4) - sub) & 7
    back = (lane + 16 * sub) & 127
    for r in range(CELL_ROWS):
        movie_ref[r * ROW : r * ROW + 8, :] = jnp.zeros((8, 128), F32)
        movie_ref[(r + 1) * ROW - 8 : (r + 1) * ROW, :] = jnp.zeros((8, 128), F32)

    def block(g, _):
        base = (1 + 8 * (g // TA)) * TA + g % TA
        for t in range(8):
            both = got_ref[g, 16 * t : 16 * t + 16, :].astype(F32)
            for h in range(2):
                value = both[8 * h : 8 * h + 8]
                value = pick_lanes(pick_rows(pick_lanes(value, skew), turn), back)
                movie_ref[pl.ds(base + (2 * t + h) * ROW, 8, stride=TA), :] = value
        high, low = [got_ref[g, 128 + 16 * at : 144 + 16 * at, :].astype(F32) for at in range(2)]
        prints_ref[pl.ds(pl.multiple_of(g * 16, 16), 16), :] = high + low
        return 0

    lax.fori_loop(0, GROUP, block, 0, unroll=2)
    own = own_lanes(sub, lane)
    found = []
    for v in range(TX):
        tails = [got_ref[v * TA + z, 160:168, :].astype(F32) for z in range(TA)]
        turned = [pltpu.roll(tail, 64, 1) for tail in tails]
        values = [tail[0:4] + (tail[4:8] + other[0:4]) for tail, other in zip(tails, turned)]
        activity = jnp.zeros((8, 128), F32)
        for f in range(4):
            rows = jnp.concatenate([value[f : f + 1] for value in values] * 2, axis=0)
            activity = jnp.where((lane >> 5) == f, pick_lanes(rows, own), activity)
        activity_ref[v] = activity
        found.append(turned[0][4:7])
    row, col, name = [jnp.concatenate([one[at : at + 1] for one in found], axis=0) for at in range(3)]
    table_ref[0:8, :] = ((row + 1) * ROW + (col + (8 * sub.astype(F32) + 1)) * TA).astype(jnp.int32)
    table_ref[8:16, :] = name.astype(jnp.int32)
    real = lane < OWNED

    def most(mask):
        count = jnp.sum(jnp.where(real & mask, 1.0, 0.0), axis=1, keepdims=True)
        return jnp.max(count, axis=0, keepdims=True).astype(jnp.int32)

    top = (most(row < 0.5) + 7) >> 3
    bottom = (OWNED - most(row > 13.5)) >> 3
    even = near_ref[0] == 0
    limits = (
        jnp.where(even, top, 0),
        jnp.where(even, 8, bottom),
        jnp.where(even, 0, bottom),
        jnp.where(even, top, 8),
        top,
        jnp.maximum(top, bottom),
    )
    line = jnp.zeros((8, 128), jnp.int32)
    for at, limit in enumerate(limits):
        line = jnp.where(lane == at, limit, line)
    table_ref[16:24, :] = line


def first_kernel(
    movie_ref, raw_ref, activity_ref, near_ref, table_ref, prints_ref, wide_ref, field_ref, up_ref, down_ref
):
    def some(q, _):
        for v in range(TX):
            rows = [raw_ref[pl.ds(v * OWNED + table_ref[8 + v, q * 8 + n], 1), :] for n in range(8)]
            prints_ref[pl.ds(pl.multiple_of(v * OWNED + q * 8, 8), 8), :] = jnp.concatenate(rows, axis=0)
        return 0

    lax.fori_loop(0, 8, some, 0)
    widen(prints_ref[...], wide_ref)
    start_field(movie_ref, field_ref)
    subtract_outer(activity_ref, wide_ref, table_ref, field_ref)
    show_edges(field_ref, near_ref, up_ref, down_ref)


def fold_updates(field_ref, wide_ref, table_ref, part_ref, first, last):
    sub, lane = iotas()

    def leaf(v, q, b):
        folded = []
        for half in range(2):
            k = q * 8 + half * 4 + b
            upper, lower = print_pair(wide_ref, v * OWNED + k, sub)
            top, bottom = patch(v, k, table_ref)
            value = upper * field_ref[top, :] + lower * field_ref[bottom, :]
            folded.append(value + pltpu.roll(value, 4, 0))
        return jnp.where(sub < 4, folded[0], folded[1])

    def eight(q, _):
        for v in range(TX):
            low = merge_lanes(leaf(v, q, 0), leaf(v, q, 1), 1, lane)
            high = merge_lanes(leaf(v, q, 2), leaf(v, q, 3), 1, lane)
            part_ref[v * 8 + q] = merge_lanes(low, high, 2, lane)
        return 0

    lax.fori_loop(first, last, eight, 0)


def early_update_kernel(
    old_ref, near_ref_in, activity_ref, wide_ref, near_ref, table_ref, field_ref, part_ref
):
    subtract_inner(activity_ref, wide_ref, table_ref, field_ref)
    add_edge(field_ref, near_ref_in, near_ref[0] == 0)
    fold_updates(field_ref, wide_ref, table_ref, part_ref, table_ref[16, 0], table_ref[16, 1])


def update_kernel(
    old_ref, early_ref, far_ref, prints_ref, wide_ref, near_ref, table_ref, out_ref, field_ref, part_ref
):
    sub, lane = iotas()
    add_edge(field_ref, far_ref, near_ref[0] != 0)
    fold_updates(field_ref, wide_ref, table_ref, part_ref, table_ref[16, 2], table_ref[16, 3])
    for v in range(TX):
        parts = [part_ref[v * 8 + q] for q in range(8)]
        for shift in (4, 8, 16):
            parts = [merge_lanes(parts[n], parts[n + 1], shift, lane) for n in range(0, len(parts), 2)]
        for g in range(GROUP):
            out_ref[g, 2 * v] = parts[0][0:4]
            out_ref[g, 2 * v + 1] = parts[0][4:8]
    squares = prints_ref[...] * prints_ref[...]
    energy = lax.dot_general(
        jnp.ones((8, 128), F32),
        squares,
        (((1,), (1,)), ((), ())),
        precision=lax.Precision.HIGHEST,
        preferred_element_type=F32,
    )
    rows = energy[:, 0:128]
    for q in range(1, 4):
        rows = jnp.where(sub == q, energy[:, 128 * q : 128 * q + 128], rows)
    for g in range(GROUP):
        out_ref[g, 16] = rows[0:4]


def trace_kernel(
    parts_ref, old_ref, movie_ref, wide_ref, near_ref, places_ref, new_ref, weight_ref, field_ref, up_ref, down_ref
):
    sub, lane = iotas()
    start_field(movie_ref, field_ref)

    def total(at):
        value = parts_ref[0, at]
        for g in range(1, GROUP):
            value = value + parts_ref[g, at]
        return value

    energy = total(16)
    own = own_lanes(sub, lane)
    for v in range(TX):
        scale = pick_lanes(jnp.broadcast_to(energy[v // 2 : v // 2 + 1], (8, 128)), own + 64 * (v % 2))
        value = jnp.maximum(old_ref[v] + jnp.concatenate([total(2 * v), total(2 * v + 1)], axis=0) / (scale + RIDGE), 0.0)
        new_ref[v] = value
        power = value * value
        power = power + pltpu.roll(power, 64, 1)
        power = power + pltpu.roll(power, 32, 1)
        power = merge_rows(power, power, 1, sub)
        power = merge_rows(power, power, 2, sub)
        weight_ref[v] = value / (power + RIDGE)
    subtract_outer(new_ref, wide_ref, places_ref, field_ref)
    show_edges(field_ref, near_ref, up_ref, down_ref)


def improve_prints(weight_ref, prints_ref, table_ref, field_ref, new_ref, first, last):
    sub, lane = iotas()

    def one(v, q):
        base = pl.multiple_of(v * OWNED + q * 8, 8)
        terms = []
        for b in range(4):
            pair = spread(weight_ref[v], q * 4 + b, sub, lane)
            for half in range(2):
                for at in patch(v, q * 8 + half * 4 + b, table_ref):
                    terms.append(pair[half] * field_ref[at, :])
        sides = []
        for n in range(4):
            low = merge_rows(terms[n], terms[4 + n], 1, sub)
            high = merge_rows(terms[8 + n], terms[12 + n], 1, sub)
            sides.append(merge_rows(low, high, 2, sub))
        step = merge_lanes(
            merge_lanes(sides[0], sides[1], 64, lane), merge_lanes(sides[2], sides[3], 64, lane), 32, lane
        )
        turned = pltpu.roll(step, 4, 0)
        dx = (lane & 32) != 0
        swapped = jnp.where(dx, pltpu.roll(turned, 32, 1), pltpu.roll(turned, 96, 1))
        step = jnp.where(dx == (sub >= 4), step, swapped)
        new_ref[pl.ds(base, 8), :] = jnp.maximum(prints_ref[pl.ds(base, 8), :] + step, 0.0)

    def eight(q, _):
        for v in range(TX):
            one(v, q)
        return 0

    lax.fori_loop(first, last, eight, 0)


def early_print_kernel(
    old_ref, near_ref_in, activity_ref, wide_ref, weight_ref, prints_ref, near_ref, table_ref, field_ref, new_ref
):
    subtract_inner(activity_ref, wide_ref, table_ref, field_ref)
    add_edge(field_ref, near_ref_in, near_ref[0] == 0)
    improve_prints(weight_ref, prints_ref, table_ref, field_ref, new_ref, table_ref[16, 0], table_ref[16, 1])


def finish_prints(far_ref, weight_ref, prints_ref, near_ref, table_ref, field_ref, new_ref):
    add_edge(field_ref, far_ref, near_ref[0] != 0)
    improve_prints(weight_ref, prints_ref, table_ref, field_ref, new_ref, table_ref[16, 2], table_ref[16, 3])


def print_kernel(
    old_ref, early_ref, far_ref, weight_ref, activity_ref, movie_ref, prints_ref, near_ref, table_ref,
    field_ref, new_ref, wide_ref, next_ref, up_ref, down_ref,
):
    finish_prints(far_ref, weight_ref, prints_ref, near_ref, table_ref, field_ref, new_ref)
    widen(new_ref[...], wide_ref)
    start_field(movie_ref, next_ref)
    subtract_outer(activity_ref, wide_ref, table_ref, next_ref)
    show_edges(next_ref, near_ref, up_ref, down_ref)


def last_kernel(
    old_ref, early_ref, far_ref, weight_ref, prints_ref, near_ref, table_ref,
    field_ref, new_ref, out_ref, raw_ref, sems,
):
    finish_prints(far_ref, weight_ref, prints_ref, near_ref, table_ref, field_ref, new_ref)
    copies = []

    def some(q, _):
        for v in range(TX):
            rows = new_ref[pl.ds(pl.multiple_of(v * OWNED + q * 8, 8), 8), :]
            for n in range(8):
                raw_ref[pl.ds(v * OWNED + table_ref[8 + v, q * 8 + n], 1), :] = rows[n : n + 1]
        return 0

    lax.fori_loop(0, 8, some, 0)
    for v in range(TX):
        for z in range(TA):
            rows = raw_ref.at[pl.ds(v * OWNED, OWNED)]
            copies.append(pltpu.make_async_copy(rows, out_ref.at[v * TA + z], sems.at[v * TA + z]))
            copies[-1].start()
    for copy in copies:
        copy.wait()


def traces_kernel(activity_ref, ranks_ref, spot_ref, out_ref):
    sub, lane = iotas()
    value = activity_ref[spot_ref[0]]
    ranks = ranks_ref[...]
    m = (ranks >> 3) * 4 + (ranks & 3)
    mine = sub == ((ranks >> 2) & 1) * 4 + spot_ref[1]
    for f in range(4):
        found = jnp.where(mine, pick_lanes(value, f * 32 + m), 0.0)
        out_ref[f : f + 1, :] = jnp.sum(found, axis=0, keepdims=True)[:, 0:OWNED]


def swap_lanes(parts, lane):
    for shift in (1, 2):
        high = (lane & (32 * shift)) != 0
        turned = []
        for b in range(4):
            other = pltpu.roll(parts[b ^ shift], 32 * shift if b & shift == 0 else 128 - 32 * shift, 1)
            turned.append(jnp.where(high, other, parts[b]) if b & shift == 0 else jnp.where(high, parts[b], other))
        parts = turned
    return parts


def finish_kernel(blocks_ref, out_ref, rows_ref, sems):
    lane = lax.broadcasted_iota(jnp.int32, (OWNED, 128), 1)
    copies = []
    for z in range(TA):
        for a in range(2):
            rows = swap_lanes([blocks_ref[(4 * a + b) * TA + z] for b in range(4)], lane)
            for d in range(4):
                at = len(copies)
                rows_ref[at] = rows[d]
                columns = pl.ds(d * 1024 + (z * 2 + a) * 128, 128)
                copies.append(pltpu.make_async_copy(rows_ref.at[at], out_ref.at[:, columns], sems.at[at]))
                copies[-1].start()
    for copy in copies:
        copy.wait()


def shape(*sizes, dtype=F32):
    return jax.ShapeDtypeStruct(sizes, dtype)


def call(kernel, outs, operands, scratch=(), smem=(), alias=(), left=(), work=1):
    return pl.pallas_call(
        kernel,
        out_shape=list(outs),
        in_specs=[SMEM if at in smem else VMEM for at in range(operands)],
        out_specs=[ANY if at in left else VMEM for at in range(len(outs))],
        scratch_shapes=list(scratch),
        input_output_aliases=dict(alias),
        compiler_params=pltpu.CompilerParams(vmem_limit_bytes=16 << 20),
        cost_estimate=pl.CostEstimate(flops=work << 20, bytes_accessed=work << 20, transcendentals=0),
    )


FIELD_SHAPE = shape(FIELD, 128)
EDGE_SHAPE = shape(2 * ROW, 128)
PRINT_SHAPE = shape(COUNT, 128)
TRACE_SHAPE = shape(TX, 8, 128)
WIDE_SHAPE = shape(4, COUNT, 128)
AXES = ("tx", "ta")


def exchange(blocks):
    return lax.all_to_all(blocks, AXES, 0, 0, tiled=True)


def halo(near, far):
    near = lax.ppermute(near, "ty", [(0, 1), (1, 0), (2, 3), (3, 2)])
    return near, lax.ppermute(far, "ty", [(1, 2), (2, 1)])


def shards(movie, footprints, traces, anchor_row, anchor_col):
    layer = lax.axis_index("ta")
    column = lax.axis_index("tx")
    frames = traces.shape[0]
    near = (lax.axis_index("ty") % 2).reshape(1)
    blocks = movie.reshape(frames, 4, CELL_ROWS, TX, 2, 128).transpose(3, 1, 2, 0, 4, 5)
    small = jnp.concatenate([traces, jnp.stack([anchor_row, anchor_col]).astype(F32)])
    sent, ranks = call(
        pack_kernel, (shape(GROUP, 168, 128, dtype=jnp.bfloat16), shape(8, 128, dtype=jnp.int32)), 4, smem=(3,)
    )(blocks.reshape(GROUP, 128, 128), footprints, small, layer.reshape(1))
    cells, raw, activity, table = call(
        unpack_kernel,
        (shape(INNER, 128), PRINT_SHAPE, TRACE_SHAPE, shape(24, 128, dtype=jnp.int32)),
        2,
        smem=(1,),
    )(exchange(sent), near)
    prints, wide, field, left, right = call(
        first_kernel, (PRINT_SHAPE, WIDE_SHAPE, FIELD_SHAPE, EDGE_SHAPE, EDGE_SHAPE), 5, smem=(3, 4)
    )(cells, raw, activity, near, table)
    for sweep in range(ITERS):
        left, right = halo(left, right)
        field, part = call(
            early_update_kernel, (FIELD_SHAPE, shape(64, 8, 128)), 6, smem=(4, 5), alias=((0, 0),), work=8
        )(field, left, activity, wide, near, table)
        sums, _, _ = call(
            update_kernel,
            (shape(GROUP, 17, 4, 128), FIELD_SHAPE, shape(64, 8, 128)),
            7,
            smem=(5, 6),
            alias=((0, 1), (1, 2)),
        )(field, part, right, prints, wide, near, table)
        activity, weight, field, left, right = call(
            trace_kernel, (TRACE_SHAPE, TRACE_SHAPE, FIELD_SHAPE, EDGE_SHAPE, EDGE_SHAPE), 6, smem=(4, 5)
        )(exchange(sums), activity, cells, wide, near, table)
        left, right = halo(left, right)
        field, new = call(early_print_kernel, (FIELD_SHAPE, PRINT_SHAPE), 8, smem=(6, 7), alias=((0, 0),), work=8)(
            field, left, activity, wide, weight, prints, near, table
        )
        if sweep + 1 < ITERS:
            _, prints, wide, field, left, right = call(
                print_kernel,
                (FIELD_SHAPE, PRINT_SHAPE, WIDE_SHAPE, FIELD_SHAPE, EDGE_SHAPE, EDGE_SHAPE),
                9,
                smem=(7, 8),
                alias=((0, 0), (1, 1)),
            )(field, new, right, weight, activity, cells, prints, near, table)
        else:
            _, _, sent = call(
                last_kernel,
                (FIELD_SHAPE, PRINT_SHAPE, shape(GROUP, OWNED, 128)),
                7,
                (pltpu.VMEM((COUNT, 128), F32), pltpu.SemaphoreType.DMA((GROUP,))),
                smem=(5, 6),
                alias=((0, 0), (1, 1)),
                left=(2,),
            )(field, new, right, weight, prints, near, table)
    footprints_out = call(
        finish_kernel,
        (shape(OWNED, 4096),),
        1,
        (pltpu.VMEM((GROUP, OWNED, 128), F32), pltpu.SemaphoreType.DMA((GROUP,))),
        left=(0,),
    )(exchange(sent))[0]
    traces_out = call(traces_kernel, (shape(4, OWNED),), 3, smem=(2,))(activity, ranks, jnp.stack([column, layer]))[0]
    return footprints_out, traces_out


def solution(mesh):
    placed = (
        P("ta", None, "ty", "tx"),
        P(("ty", "tx"), None),
        P("ta", ("ty", "tx")),
        P(("ty", "tx")),
        P(("ty", "tx")),
    )
    return jax.shard_map(
        shards,
        mesh=mesh,
        in_specs=placed,
        out_specs=(P(("ty", "tx"), None), P("ta", ("ty", "tx"))),
        check_vma=False,
    )
```

```python
import functools

import jax
import jax.numpy as jnp
from jax import lax
from jax.experimental import pallas as pl
from jax.experimental.pallas import tpu as pltpu
from jax.sharding import PartitionSpec as P

ITERS = 2
RIDGE = 1.0
TX = 8
TA = 4
GROUP = TX * TA
OWNED = 64
COUNT = TX * OWNED
ROW = (TX * 8 + 2) * TA
CELL_ROWS = 16
FIELD = (CELL_ROWS + 2) * ROW
INNER = CELL_ROWS * ROW
VMEM = pl.BlockSpec(memory_space=pltpu.VMEM)
SMEM = pl.BlockSpec(memory_space=pltpu.SMEM)
ANY = pl.BlockSpec(memory_space=pl.ANY)
F32 = jnp.float32


def iotas():
    return (
        lax.broadcasted_iota(jnp.int32, (8, 128), 0),
        lax.broadcasted_iota(jnp.int32, (8, 128), 1),
    )


def pick_lanes(value, index):
    return jnp.take_along_axis(value, index, axis=1, mode="promise_in_bounds")


def pick_rows(value, index):
    return jnp.take_along_axis(value, index, axis=0, mode="promise_in_bounds")


def merge_lanes(first, second, shift, lane):
    if shift == 64:
        high = lane >= 64
        return jnp.where(high, second, first) + pltpu.roll(jnp.where(high, first, second), 64, 1)
    return jnp.where(
        (lane & shift) != 0,
        second + pltpu.roll(second, shift, 1),
        first + pltpu.roll(first, 128 - shift, 1),
    )


def merge_rows(first, second, shift, sub):
    return jnp.where(
        (sub & shift) != 0,
        second + pltpu.roll(second, shift, 0),
        first + pltpu.roll(first, 8 - shift, 0),
    )


def spread(value, m, sub, lane):
    wide = pick_lanes(value, (lane & 96) + m)
    turned = pltpu.roll(wide, 4, 0)
    low = sub < 4
    return jnp.where(low, wide, turned), jnp.where(low, turned, wide)


def pieces(value, count):
    out = []
    for _ in range(count):
        out.append(value.astype(jnp.bfloat16))
        value = value - out[-1].astype(F32)
    return out


def widen(prints, wide_ref):
    source = lax.broadcasted_iota(jnp.int32, (384, 512), 0) & 127
    target = lax.broadcasted_iota(jnp.int32, (384, 512), 1)
    copies = (source == (target >> 7) * 32 + (target & 31)).astype(jnp.bfloat16)
    parts = jnp.concatenate(pieces(prints, 3), axis=1)
    wide = jnp.dot(parts, copies, preferred_element_type=F32)
    for d in range(4):
        wide_ref[d] = wide[:, 128 * d : 128 * d + 128]


def print_pair(wide_ref, neuron, sub):
    rows = [jnp.broadcast_to(wide_ref[d, pl.ds(neuron, 1), :], (8, 128)) for d in range(4)]
    return jnp.where(sub < 4, rows[0], rows[1]), jnp.where(sub < 4, rows[2], rows[3])


def patch(v, k, places_ref):
    start = pl.multiple_of(places_ref[v, k], 4)
    return pl.ds(start, 8), pl.ds(start + ROW, 8)


def subtract_some(activity_ref, wide_ref, table_ref, field_ref, count, group_of):
    sub, lane = iotas()
    for first in range(2):
        tiles = [first + 2 * t for t in range(4)]
        values = [activity_ref[v] for v in tiles]

        def some(at, _):
            q = group_of(at)
            for b in range(4):
                pairs = [spread(value, q * 4 + b, sub, lane) for value in values]
                for half in range(2):
                    spots, changed = [], []
                    for v, pair in zip(tiles, pairs):
                        k = q * 8 + half * 4 + b
                        for at, side in zip(patch(v, k, table_ref), print_pair(wide_ref, v * OWNED + k, sub)):
                            spots.append(at)
                            changed.append(field_ref[at, :] - pair[half] * side)
                    for at, value in zip(spots, changed):
                        field_ref[at, :] = value
            return 0

        lax.fori_loop(0, count, some, 0)


def subtract_outer(activity_ref, wide_ref, table_ref, field_ref):
    start, stop = table_ref[16, 4], table_ref[16, 5]
    subtract_some(
        activity_ref,
        wide_ref,
        table_ref,
        field_ref,
        start + 8 - stop,
        lambda at: at + jnp.where(at >= start, stop - start, 0),
    )


def subtract_inner(activity_ref, wide_ref, table_ref, field_ref):
    start, stop = table_ref[16, 4], table_ref[16, 5]
    subtract_some(activity_ref, wide_ref, table_ref, field_ref, stop - start, lambda at: at + start)


def start_field(movie_ref, field_ref):
    field_ref[0:ROW, :] = jnp.zeros((ROW, 128), F32)
    field_ref[ROW + INNER :, :] = jnp.zeros((ROW, 128), F32)

    def one(r, _):
        field_ref[pl.ds((r + 1) * ROW, ROW), :] = movie_ref[pl.ds(r * ROW, ROW), :]
        return 0

    lax.fori_loop(0, CELL_ROWS, one, 0)


def add_edge(field_ref, edge_ref, low):
    rows = pl.ds(pl.multiple_of(jnp.where(low, INNER, 0), 8), 2 * ROW)
    field_ref[rows, :] += edge_ref[...]


def show_edges(field_ref, near_ref, near_out, far_out):
    even = near_ref[0] == 0
    top = field_ref[0 : 2 * ROW, :]
    bottom = field_ref[INNER:, :]
    near_out[...] = jnp.where(even, bottom, top)
    far_out[...] = jnp.where(even, top, bottom)


def pack_kernel(cells_ref, prints_ref, small_ref, layer_ref, out_ref, ranks_ref):
    lane = lax.broadcasted_iota(jnp.int32, (16, 128), 1)
    rows = pl.ds(pl.multiple_of(layer_ref[0] * 16, 16), 16)
    down = lax.broadcasted_iota(jnp.int32, (OWNED, OWNED), 0)
    right = lax.broadcasted_iota(jnp.int32, (OWNED, OWNED), 1)
    theirs = jnp.broadcast_to(small_ref[4:5, :], (OWNED, OWNED))
    ours = dot((down == right).astype(F32), theirs, 1)
    before = (theirs < ours) | ((theirs == ours) & (right < down))
    ranks = jnp.sum(before.astype(F32), axis=1, keepdims=True).astype(jnp.int32)
    order = (right == ranks).astype(F32)
    names = right[0:1].astype(F32)
    tail = [piece.astype(F32) for piece in pieces(small_ref[0:4, :], 3)]
    tail = dot(jnp.concatenate(tail + [small_ref[4:6, :], names, jnp.zeros((1, OWNED), F32)], axis=0), order, 0)
    tail = jnp.concatenate([tail[0:8], tail[8:16]], axis=1)
    tail = jnp.concatenate([tail, tail], axis=0).astype(jnp.bfloat16)
    places = dot(jnp.broadcast_to(names, (8, OWNED)), order, 1)
    ranks_ref[...] = jnp.concatenate([places, jnp.zeros((8, OWNED), F32)], axis=1).astype(jnp.int32)
    for a in range(8):
        blocks = swap_lanes(
            [prints_ref[rows, d * 1024 + a * 128 : d * 1024 + a * 128 + 128] for d in range(4)], lane
        )
        for b in range(4):
            shard = 4 * a + b
            dest = (shard % TX) * TA + shard // TX
            out_ref[dest, 0:128, :] = cells_ref[dest]
            for at, piece in enumerate(pieces(blocks[b], 2)):
                out_ref[dest, 128 + 16 * at : 144 + 16 * at, :] = piece
            out_ref[dest, 160:168, :] = tail[0:8]


def dot(left, right, axis):
    return lax.dot_general(left, right, (((1,), (axis,)), ((), ())), preferred_element_type=F32)


def own_lanes(sub, lane):
    m = lane & 31
    return (m >> 2) * 8 + (m & 3) + jnp.where(sub < 4, 0, 4)


def unpack_kernel(got_ref, near_ref, movie_ref, prints_ref, activity_ref, table_ref):
    sub, lane = iotas()
    skew = (lane - 16 * sub) & 127
    turn = ((lane >> 4) - sub) & 7
    back = (lane + 16 * sub) & 127
    for r in range(CELL_ROWS):
        movie_ref[r * ROW : r * ROW + 8, :] = jnp.zeros((8, 128), F32)
        movie_ref[(r + 1) * ROW - 8 : (r + 1) * ROW, :] = jnp.zeros((8, 128), F32)

    def block(g, _):
        base = (1 + 8 * (g // TA)) * TA + g % TA
        for t in range(8):
            both = got_ref[g, 16 * t : 16 * t + 16, :].astype(F32)
            for h in range(2):
                value = both[8 * h : 8 * h + 8]
                value = pick_lanes(pick_rows(pick_lanes(value, skew), turn), back)
                movie_ref[pl.ds(base + (2 * t + h) * ROW, 8, stride=TA), :] = value
        high, low = [got_ref[g, 128 + 16 * at : 144 + 16 * at, :].astype(F32) for at in range(2)]
        prints_ref[pl.ds(pl.multiple_of(g * 16, 16), 16), :] = high + low
        return 0

    lax.fori_loop(0, GROUP, block, 0, unroll=2)
    own = own_lanes(sub, lane)
    found = []
    for v in range(TX):
        tails = [got_ref[v * TA + z, 160:168, :].astype(F32) for z in range(TA)]
        turned = [pltpu.roll(tail, 64, 1) for tail in tails]
        values = [tail[0:4] + (tail[4:8] + other[0:4]) for tail, other in zip(tails, turned)]
        activity = jnp.zeros((8, 128), F32)
        for f in range(4):
            rows = jnp.concatenate([value[f : f + 1] for value in values] * 2, axis=0)
            activity = jnp.where((lane >> 5) == f, pick_lanes(rows, own), activity)
        activity_ref[v] = activity
        found.append(turned[0][4:7])
    row, col, name = [jnp.concatenate([one[at : at + 1] for one in found], axis=0) for at in range(3)]
    table_ref[0:8, :] = ((row + 1) * ROW + (col + (8 * sub.astype(F32) + 1)) * TA).astype(jnp.int32)
    table_ref[8:16, :] = name.astype(jnp.int32)
    real = lane < OWNED

    def most(mask):
        count = jnp.sum(jnp.where(real & mask, 1.0, 0.0), axis=1, keepdims=True)
        return jnp.max(count, axis=0, keepdims=True).astype(jnp.int32)

    top = (most(row < 0.5) + 7) >> 3
    bottom = (OWNED - most(row > 13.5)) >> 3
    even = near_ref[0] == 0
    limits = (
        jnp.where(even, top, 0),
        jnp.where(even, 8, bottom),
        jnp.where(even, 0, bottom),
        jnp.where(even, top, 8),
        top,
        jnp.maximum(top, bottom),
    )
    line = jnp.zeros((8, 128), jnp.int32)
    for at, limit in enumerate(limits):
        line = jnp.where(lane == at, limit, line)
    table_ref[16:24, :] = line


def first_kernel(
    movie_ref, raw_ref, activity_ref, near_ref, table_ref, prints_ref, wide_ref, field_ref, up_ref, down_ref
):
    def some(q, _):
        for v in range(TX):
            rows = [raw_ref[pl.ds(v * OWNED + table_ref[8 + v, q * 8 + n], 1), :] for n in range(8)]
            prints_ref[pl.ds(pl.multiple_of(v * OWNED + q * 8, 8), 8), :] = jnp.concatenate(rows, axis=0)
        return 0

    lax.fori_loop(0, 8, some, 0)
    widen(prints_ref[...], wide_ref)
    start_field(movie_ref, field_ref)
    subtract_outer(activity_ref, wide_ref, table_ref, field_ref)
    show_edges(field_ref, near_ref, up_ref, down_ref)


def fold_updates(field_ref, wide_ref, table_ref, part_ref, first, last):
    sub, lane = iotas()

    def leaf(v, q, b):
        folded = []
        for half in range(2):
            k = q * 8 + half * 4 + b
            upper, lower = print_pair(wide_ref, v * OWNED + k, sub)
            top, bottom = patch(v, k, table_ref)
            value = upper * field_ref[top, :] + lower * field_ref[bottom, :]
            folded.append(value + pltpu.roll(value, 4, 0))
        return jnp.where(sub < 4, folded[0], folded[1])

    def eight(q, _):
        for v in range(TX):
            low = merge_lanes(leaf(v, q, 0), leaf(v, q, 1), 1, lane)
            high = merge_lanes(leaf(v, q, 2), leaf(v, q, 3), 1, lane)
            part_ref[v * 8 + q] = merge_lanes(low, high, 2, lane)
        return 0

    lax.fori_loop(first, last, eight, 0)


def early_update_kernel(
    old_ref, near_ref_in, activity_ref, prints_ref, wide_ref, near_ref, table_ref, field_ref, part_ref, energy_ref
):
    sub, lane = iotas()
    squares = prints_ref[...] * prints_ref[...]
    energy = lax.dot_general(
        jnp.ones((8, 128), F32),
        squares,
        (((1,), (1,)), ((), ())),
        precision=lax.Precision.HIGHEST,
        preferred_element_type=F32,
    )
    rows = energy[:, 0:128]
    for q in range(1, 4):
        rows = jnp.where(sub == q, energy[:, 128 * q : 128 * q + 128], rows)
    energy_ref[...] = rows
    subtract_inner(activity_ref, wide_ref, table_ref, field_ref)
    add_edge(field_ref, near_ref_in, near_ref[0] == 0)
    fold_updates(field_ref, wide_ref, table_ref, part_ref, table_ref[16, 0], table_ref[16, 1])


def update_kernel(
    old_ref, early_ref, far_ref, energy_ref, wide_ref, near_ref, table_ref, out_ref, field_ref, part_ref
):
    sub, lane = iotas()
    add_edge(field_ref, far_ref, near_ref[0] != 0)
    fold_updates(field_ref, wide_ref, table_ref, part_ref, table_ref[16, 2], table_ref[16, 3])
    for v in range(TX):
        parts = [part_ref[v * 8 + q] for q in range(8)]
        for shift in (4, 8, 16):
            parts = [merge_lanes(parts[n], parts[n + 1], shift, lane) for n in range(0, len(parts), 2)]
        for g in range(GROUP):
            out_ref[g, 2 * v] = parts[0][0:4]
            out_ref[g, 2 * v + 1] = parts[0][4:8]
    rows = energy_ref[...]
    for g in range(GROUP):
        out_ref[g, 16] = rows[0:4]


def trace_kernel(
    parts_ref, old_ref, movie_ref, wide_ref, near_ref, places_ref, new_ref, weight_ref, field_ref, up_ref, down_ref
):
    sub, lane = iotas()
    start_field(movie_ref, field_ref)

    def total(at):
        value = parts_ref[0, at]
        for g in range(1, GROUP):
            value = value + parts_ref[g, at]
        return value

    energy = total(16)
    own = own_lanes(sub, lane)
    for v in range(TX):
        scale = pick_lanes(jnp.broadcast_to(energy[v // 2 : v // 2 + 1], (8, 128)), own + 64 * (v % 2))
        value = jnp.maximum(old_ref[v] + jnp.concatenate([total(2 * v), total(2 * v + 1)], axis=0) / (scale + RIDGE), 0.0)
        new_ref[v] = value
        power = value * value
        power = power + pltpu.roll(power, 64, 1)
        power = power + pltpu.roll(power, 32, 1)
        power = merge_rows(power, power, 1, sub)
        power = merge_rows(power, power, 2, sub)
        weight_ref[v] = value / (power + RIDGE)
    subtract_outer(new_ref, wide_ref, places_ref, field_ref)
    show_edges(field_ref, near_ref, up_ref, down_ref)


def improve_prints(weight_ref, prints_ref, table_ref, field_ref, new_ref, first, last):
    sub, lane = iotas()

    def one(v, q):
        base = pl.multiple_of(v * OWNED + q * 8, 8)
        terms = []
        for b in range(4):
            pair = spread(weight_ref[v], q * 4 + b, sub, lane)
            for half in range(2):
                for at in patch(v, q * 8 + half * 4 + b, table_ref):
                    terms.append(pair[half] * field_ref[at, :])
        sides = []
        for n in range(4):
            low = merge_rows(terms[n], terms[4 + n], 1, sub)
            high = merge_rows(terms[8 + n], terms[12 + n], 1, sub)
            sides.append(merge_rows(low, high, 2, sub))
        step = merge_lanes(
            merge_lanes(sides[0], sides[1], 64, lane), merge_lanes(sides[2], sides[3], 64, lane), 32, lane
        )
        turned = pltpu.roll(step, 4, 0)
        dx = (lane & 32) != 0
        swapped = jnp.where(dx, pltpu.roll(turned, 32, 1), pltpu.roll(turned, 96, 1))
        step = jnp.where(dx == (sub >= 4), step, swapped)
        new_ref[pl.ds(base, 8), :] = jnp.maximum(prints_ref[pl.ds(base, 8), :] + step, 0.0)

    def eight(q, _):
        for v in range(TX):
            one(v, q)
        return 0

    lax.fori_loop(first, last, eight, 0)


def early_print_kernel(
    old_ref, near_ref_in, activity_ref, wide_ref, weight_ref, prints_ref, near_ref, table_ref, field_ref, new_ref
):
    subtract_inner(activity_ref, wide_ref, table_ref, field_ref)
    add_edge(field_ref, near_ref_in, near_ref[0] == 0)
    improve_prints(weight_ref, prints_ref, table_ref, field_ref, new_ref, table_ref[16, 0], table_ref[16, 1])


def finish_prints(far_ref, weight_ref, prints_ref, near_ref, table_ref, field_ref, new_ref):
    add_edge(field_ref, far_ref, near_ref[0] != 0)
    improve_prints(weight_ref, prints_ref, table_ref, field_ref, new_ref, table_ref[16, 2], table_ref[16, 3])


def print_kernel(
    old_ref, early_ref, far_ref, weight_ref, activity_ref, movie_ref, prints_ref, near_ref, table_ref,
    field_ref, new_ref, wide_ref, next_ref, up_ref, down_ref,
):
    finish_prints(far_ref, weight_ref, prints_ref, near_ref, table_ref, field_ref, new_ref)
    widen(new_ref[...], wide_ref)
    start_field(movie_ref, next_ref)
    subtract_outer(activity_ref, wide_ref, table_ref, next_ref)
    show_edges(next_ref, near_ref, up_ref, down_ref)


def last_kernel(
    old_ref, early_ref, far_ref, weight_ref, prints_ref, near_ref, table_ref,
    field_ref, new_ref, out_ref, raw_ref, sems,
):
    finish_prints(far_ref, weight_ref, prints_ref, near_ref, table_ref, field_ref, new_ref)
    copies = []

    def some(q, _):
        for v in range(TX):
            rows = new_ref[pl.ds(pl.multiple_of(v * OWNED + q * 8, 8), 8), :]
            for n in range(8):
                raw_ref[pl.ds(v * OWNED + table_ref[8 + v, q * 8 + n], 1), :] = rows[n : n + 1]
        return 0

    lax.fori_loop(0, 8, some, 0)
    for v in range(TX):
        for z in range(TA):
            rows = raw_ref.at[pl.ds(v * OWNED, OWNED)]
            copies.append(pltpu.make_async_copy(rows, out_ref.at[v * TA + z], sems.at[v * TA + z]))
            copies[-1].start()
    for copy in copies:
        copy.wait()


def traces_kernel(activity_ref, ranks_ref, spot_ref, out_ref):
    sub, lane = iotas()
    value = activity_ref[spot_ref[0]]
    ranks = ranks_ref[...]
    m = (ranks >> 3) * 4 + (ranks & 3)
    mine = sub == ((ranks >> 2) & 1) * 4 + spot_ref[1]
    for f in range(4):
        found = jnp.where(mine, pick_lanes(value, f * 32 + m), 0.0)
        out_ref[f : f + 1, :] = jnp.sum(found, axis=0, keepdims=True)[:, 0:OWNED]


def swap_lanes(parts, lane):
    for shift in (1, 2):
        high = (lane & (32 * shift)) != 0
        turned = []
        for b in range(4):
            other = pltpu.roll(parts[b ^ shift], 32 * shift if b & shift == 0 else 128 - 32 * shift, 1)
            turned.append(jnp.where(high, other, parts[b]) if b & shift == 0 else jnp.where(high, parts[b], other))
        parts = turned
    return parts


def finish_kernel(blocks_ref, out_ref, rows_ref, sems):
    lane = lax.broadcasted_iota(jnp.int32, (OWNED, 128), 1)
    copies = []
    for z in range(TA):
        for a in range(2):
            rows = swap_lanes([blocks_ref[(4 * a + b) * TA + z] for b in range(4)], lane)
            for d in range(4):
                at = len(copies)
                rows_ref[at] = rows[d]
                columns = pl.ds(d * 1024 + (z * 2 + a) * 128, 128)
                copies.append(pltpu.make_async_copy(rows_ref.at[at], out_ref.at[:, columns], sems.at[at]))
                copies[-1].start()
    for copy in copies:
        copy.wait()


def shape(*sizes, dtype=F32):
    return jax.ShapeDtypeStruct(sizes, dtype)


def call(kernel, outs, operands, scratch=(), smem=(), alias=(), left=(), work=1):
    return pl.pallas_call(
        kernel,
        out_shape=list(outs),
        in_specs=[SMEM if at in smem else VMEM for at in range(operands)],
        out_specs=[ANY if at in left else VMEM for at in range(len(outs))],
        scratch_shapes=list(scratch),
        input_output_aliases=dict(alias),
        compiler_params=pltpu.CompilerParams(vmem_limit_bytes=16 << 20),
        cost_estimate=pl.CostEstimate(flops=work << 20, bytes_accessed=work << 20, transcendentals=0),
    )


FIELD_SHAPE = shape(FIELD, 128)
EDGE_SHAPE = shape(2 * ROW, 128)
PRINT_SHAPE = shape(COUNT, 128)
TRACE_SHAPE = shape(TX, 8, 128)
WIDE_SHAPE = shape(4, COUNT, 128)
AXES = ("tx", "ta")


def exchange(blocks):
    return lax.all_to_all(blocks, AXES, 0, 0, tiled=True)


def halo(near, far):
    near = lax.ppermute(near, "ty", [(0, 1), (1, 0), (2, 3), (3, 2)])
    return near, lax.ppermute(far, "ty", [(1, 2), (2, 1)])


def shards(movie, footprints, traces, anchor_row, anchor_col):
    layer = lax.axis_index("ta")
    column = lax.axis_index("tx")
    frames = traces.shape[0]
    near = (lax.axis_index("ty") % 2).reshape(1)
    blocks = movie.reshape(frames, 4, CELL_ROWS, TX, 2, 128).transpose(3, 1, 2, 0, 4, 5)
    small = jnp.concatenate([traces, jnp.stack([anchor_row, anchor_col]).astype(F32)])
    sent, ranks = call(
        pack_kernel, (shape(GROUP, 168, 128, dtype=jnp.bfloat16), shape(8, 128, dtype=jnp.int32)), 4, smem=(3,)
    )(blocks.reshape(GROUP, 128, 128), footprints, small, layer.reshape(1))
    cells, raw, activity, table = call(
        unpack_kernel,
        (shape(INNER, 128), PRINT_SHAPE, TRACE_SHAPE, shape(24, 128, dtype=jnp.int32)),
        2,
        smem=(1,),
    )(exchange(sent), near)
    prints, wide, field, left, right = call(
        first_kernel, (PRINT_SHAPE, WIDE_SHAPE, FIELD_SHAPE, EDGE_SHAPE, EDGE_SHAPE), 5, smem=(3, 4)
    )(cells, raw, activity, near, table)
    for sweep in range(ITERS):
        left, right = halo(left, right)
        field, part, energy = call(
            early_update_kernel,
            (FIELD_SHAPE, shape(64, 8, 128), shape(8, 128)),
            7,
            smem=(5, 6),
            alias=((0, 0),),
            work=8,
        )(field, left, activity, prints, wide, near, table)
        sums, _, _ = call(
            update_kernel,
            (shape(GROUP, 17, 4, 128), FIELD_SHAPE, shape(64, 8, 128)),
            7,
            smem=(5, 6),
            alias=((0, 1), (1, 2)),
        )(field, part, right, energy, wide, near, table)
        activity, weight, field, left, right = call(
            trace_kernel, (TRACE_SHAPE, TRACE_SHAPE, FIELD_SHAPE, EDGE_SHAPE, EDGE_SHAPE), 6, smem=(4, 5)
        )(exchange(sums), activity, cells, wide, near, table)
        left, right = halo(left, right)
        field, new = call(early_print_kernel, (FIELD_SHAPE, PRINT_SHAPE), 8, smem=(6, 7), alias=((0, 0),), work=8)(
            field, left, activity, wide, weight, prints, near, table
        )
        if sweep + 1 < ITERS:
            _, prints, wide, field, left, right = call(
                print_kernel,
                (FIELD_SHAPE, PRINT_SHAPE, WIDE_SHAPE, FIELD_SHAPE, EDGE_SHAPE, EDGE_SHAPE),
                9,
                smem=(7, 8),
                alias=((0, 0), (1, 1)),
            )(field, new, right, weight, activity, cells, prints, near, table)
        else:
            _, _, sent = call(
                last_kernel,
                (FIELD_SHAPE, PRINT_SHAPE, shape(GROUP, OWNED, 128)),
                7,
                (pltpu.VMEM((COUNT, 128), F32), pltpu.SemaphoreType.DMA((GROUP,))),
                smem=(5, 6),
                alias=((0, 0), (1, 1)),
                left=(2,),
            )(field, new, right, weight, prints, near, table)
    footprints_out = call(
        finish_kernel,
        (shape(OWNED, 4096),),
        1,
        (pltpu.VMEM((GROUP, OWNED, 128), F32), pltpu.SemaphoreType.DMA((GROUP,))),
        left=(0,),
    )(exchange(sent))[0]
    traces_out = call(traces_kernel, (shape(4, OWNED),), 3, smem=(2,))(activity, ranks, jnp.stack([column, layer]))[0]
    return footprints_out, traces_out


def solution(mesh):
    placed = (
        P("ta", None, "ty", "tx"),
        P(("ty", "tx"), None),
        P("ta", ("ty", "tx")),
        P(("ty", "tx")),
        P(("ty", "tx")),
    )
    return jax.shard_map(
        shards,
        mesh=mesh,
        in_specs=placed,
        out_specs=(P(("ty", "tx"), None), P("ta", ("ty", "tx"))),
        check_vma=False,
    )
```
